128 devices in a mesh: visit: 8 (over x, core), patch: 16 (over y, z).
Axes of the slice: x: 4, y: 4, z: 4, core: 2. Of those that a mesh axis runs over, the one named last changes fastest.
Arguments:
- images: bfloat16 [1024, 512, 512], P(('visit', 'patch')), may hold values from -10 to 10
- warp_rows: bfloat16 [1024, 512, 512], P(('visit', 'patch')), may hold values from -2 to 2
- warp_cols: bfloat16 [1024, 512, 512], P(('visit', 'patch')), may hold values from -2 to 2
- tile_weight: bfloat16 [1024], P(('visit', 'patch')), may hold values from 0.5 to 4
- tile_patch: int32 [1024], P(('visit', 'patch')), may hold values from 0 to 15, as said below
- match_rows: float32 [16, 512, 512], P('patch'), may hold values from -2 to 2
- match_cols: float32 [16, 512, 512], P('patch'), may hold values from -2 to 2
- src_row: int32 [16, 512], P('patch'), may hold values from 0 to 511
- src_col: int32 [16, 512], P('patch'), may hold values from 0 to 511
Outputs:
- coadd: float32 [16, 512, 512], P('patch', 'visit')
- zero_point: float32 [32], P('visit')
- flux_resid: float32 [1024, 512], P(('visit', 'patch'))
The draws below stay inside these ranges and needn't reach their ends.
Inputs may be any that keep to these rules, and one draw needn't show every extreme that they name: `tile_patch`: among the 8 tiles of one device no patch is named more than 2 times; in each visit row one patch is named exactly 2 times by every device of the row; every patch is named by some tile of every visit row.
All inputs are finite; a program needn't handle non-finite values.
Results may differ from the reference program's by a relative error of at most 0.0065.
Values may be sent and summed in bfloat16 or wider, within the bound.
A program may use at most 128 MiB of HBM per device.

```python
import math
import jax
import jax.numpy as jnp
from jax import lax

S = 512
TILES_DEV = 8
VIS_ROW = 4
CAP = 2
SRC = 512
TILES = 1024
PATCHES = 16
VISITS = 32
N_VISIT = 8
N_PATCH = 16


def route_table(key):
    devices_all = N_VISIT * N_PATCH
    hot_key, score_key, order_key = jax.random.split(jax.random.fold_in(key, 11), 3)
    hot_patch = jnp.repeat(jax.random.randint(hot_key, (N_VISIT,), 0, N_PATCH), N_PATCH)
    own_patch = jnp.tile(jnp.arange(N_PATCH), N_VISIT)
    places = jnp.arange(2 * N_PATCH)
    candidates = places % N_PATCH
    scores = jax.random.randint(score_key, (devices_all, 2 * N_PATCH), 0, 2 ** 20) * 128 + places[None, :]
    forced = (candidates[None, :] == own_patch[:, None]) & (places[None, :] < N_PATCH)
    scores = jnp.where(forced, scores + 2 ** 28, scores)
    scores = jnp.where(candidates[None, :] == hot_patch[:, None], -2 ** 29, scores)
    ranking = jnp.argsort(-scores, axis=1)
    chosen = candidates[ranking[:, :TILES_DEV - CAP]]
    routes = jnp.concatenate([jnp.repeat(hot_patch[:, None], CAP, axis=1), chosen], axis=1)
    mixing = jax.random.randint(order_key, (devices_all, TILES_DEV), 0, 2 ** 20) * 64 + jnp.arange(TILES_DEV)[None, :]
    routes = jnp.take_along_axis(routes, jnp.argsort(mixing, axis=1), axis=1)
    return routes.reshape(-1).astype(jnp.int32)


def draw_tile_patch(key, part):
    return route_table(key)


def draw_images(key, part):
    routes = route_table(key)
    sky_key, gain_key, noise_key = jax.random.split(jax.random.fold_in(key, 23), 3)
    tile_index = jnp.arange(TILES)
    visit_id = tile_index // (TILES_DEV * N_PATCH) * VIS_ROW + tile_index % TILES_DEV % VIS_ROW
    gains = jnp.exp(jax.random.uniform(gain_key, (VISITS,), minval=-0.7, maxval=0.7))
    sky = jnp.clip(jax.random.normal(sky_key, (N_PATCH, S, S)), -4.0, 4.0)
    noise = 0.5 * jnp.clip(jax.random.normal(noise_key, (TILES, S, S)), -4.0, 4.0)
    return (gains[visit_id][:, None, None] * sky[routes] + noise).astype(jnp.bfloat16)


def near_identity(key, count, spread):
    spread_part = jnp.clip(jax.random.normal(key, (count, S, S)), -4.0, 4.0)
    return jnp.eye(S)[None, :, :] + spread * spread_part / jnp.sqrt(S * 1.0)


def draw_warp_rows(key, part):
    return near_identity(jax.random.fold_in(key, 31), TILES, 0.4).astype(jnp.bfloat16)


def draw_warp_cols(key, part):
    return near_identity(jax.random.fold_in(key, 37), TILES, 0.4).astype(jnp.bfloat16)


def draw_match_rows(key, part):
    return near_identity(jax.random.fold_in(key, 41), PATCHES, 0.3).astype(jnp.float32)


def draw_match_cols(key, part):
    return near_identity(jax.random.fold_in(key, 43), PATCHES, 0.3).astype(jnp.float32)


def with_ends(array, own_key, least, high):
    shape = array.shape
    spot = [jax.random.randint(jax.random.fold_in(own_key, axis), (), 0, shape[axis]) for axis in range(len(shape))]
    array = array.at[tuple(spot)].set(least)
    longest = shape.index(max(shape))
    spot[longest] = (spot[longest] + 1) % shape[longest]
    return array.at[tuple(spot)].set(high)


def level_of(rng, shape, pieces, smallest, high):
    def one(dim, parts):
        draws = jax.random.uniform(jax.random.fold_in(jax.random.fold_in(rng, 6), dim), (parts,), jnp.float32, smallest / len(pieces), high / len(pieces))
        return jnp.repeat(jnp.exp(draws), shape[dim] // parts).reshape((-1,) + (1,) * (len(shape) - dim - 1))

    level = one(*pieces[0])
    for cut in pieces[1:]:
        level = level * one(*cut)
    return level


def setup_inputs(seed: int = 0) -> dict:
    seeds = jax.random.split(jax.random.key(seed), 10)
    images = draw_images(jax.random.fold_in(seeds[9], 71), 0)
    warp_rows = draw_warp_rows(jax.random.fold_in(seeds[9], 71), 0)
    warp_cols = draw_warp_cols(jax.random.fold_in(seeds[9], 71), 0)
    tile_weight = jnp.clip(jnp.exp(math.log(4.0) - 2.0794415 * jax.random.uniform(seeds[3], (TILES,), jnp.float32) ** level_of(seeds[3], (TILES,), ((0, 128),), -0.2, 0.2)), 0.5, 4.0).astype(jnp.bfloat16)
    tile_patch = draw_tile_patch(jax.random.fold_in(seeds[9], 71), 0)
    match_rows = draw_match_rows(jax.random.fold_in(seeds[9], 71), 0)
    match_cols = draw_match_cols(jax.random.fold_in(seeds[9], 71), 0)
    src_row = with_ends(jax.random.randint(seeds[7], (PATCHES, SRC), 0, S), jax.random.fold_in(seeds[7], 1), 0, S - 1).astype(jnp.int32)
    src_col = with_ends(jax.random.randint(seeds[8], (PATCHES, SRC), 0, S), jax.random.fold_in(seeds[8], 1), 0, S - 1).astype(jnp.int32)
    return dict(images=images, warp_rows=warp_rows, warp_cols=warp_cols, tile_weight=tile_weight, tile_patch=tile_patch, match_rows=match_rows, match_cols=match_cols, src_row=src_row, src_col=src_col)


HIGHEST = lax.Precision.HIGHEST
APERTURE = 2.5


def profiles(centers, length):
    pixel_grid = jnp.arange(length).astype(jnp.float32)
    distance = pixel_grid[None, :] - centers.astype(jnp.float32)[:, None]
    return jnp.exp(-distance * distance / (2.0 * APERTURE * APERTURE)).astype(jnp.bfloat16)


def reference(images, warp_rows, warp_cols, tile_weight, tile_patch, match_rows, match_cols, src_row, src_col):
    def warp_one(member):
        detector, row_matrix, col_matrix = member
        half_warp = jnp.dot(detector, col_matrix.T, preferred_element_type=jnp.float32).astype(jnp.bfloat16)
        return jnp.dot(row_matrix, half_warp, preferred_element_type=jnp.float32).astype(jnp.bfloat16)

    warped = lax.map(warp_one, (images, warp_rows, warp_cols))
    weights = tile_weight.astype(jnp.float32)

    def add_tile(running, member):
        tile_data, weight, patch_id = member
        return running.at[patch_id].add(weight * tile_data.astype(jnp.float32)), None

    stacked, _ = lax.scan(add_tile, jnp.zeros((PATCHES, S, S), jnp.float32), (warped, weights, tile_patch))
    total_weight = jax.ops.segment_sum(weights, tile_patch, PATCHES)
    matched = jnp.einsum('pij,pjk->pik', match_rows, stacked, precision=HIGHEST)
    matched = jnp.einsum('pik,plk->pil', matched, match_cols, precision=HIGHEST)
    coadd = matched / total_weight[:, None, None]
    row_prof = jax.vmap(lambda centers: profiles(centers, S))(src_row)
    col_prof = jax.vmap(lambda centers: profiles(centers, S))(src_col)
    by_column = jnp.einsum('pyx,pqx->pyq', coadd, col_prof.astype(jnp.float32), precision=HIGHEST)
    ref_flux = jnp.einsum('pyq,pqy->pq', by_column, row_prof.astype(jnp.float32), precision=HIGHEST)

    def measure(member):
        tile_data, patch_id = member
        tile_cols = jnp.dot(tile_data, col_prof[patch_id].T, preferred_element_type=jnp.float32)
        return jnp.einsum('yq,qy->q', tile_cols, row_prof[patch_id].astype(jnp.float32), precision=HIGHEST)

    fluxes = lax.map(measure, (warped, tile_patch))
    tile_ref = ref_flux[tile_patch]
    tile_index = jnp.arange(TILES)
    visit_id = (tile_index // (TILES_DEV * N_PATCH)) * VIS_ROW + (tile_index % TILES_DEV) % VIS_ROW
    numerator = jax.ops.segment_sum(jnp.sum(fluxes * tile_ref, axis=1), visit_id, VISITS)
    denominator = jax.ops.segment_sum(jnp.sum(tile_ref * tile_ref, axis=1), visit_id, VISITS)
    zero_point = numerator / denominator
    flux_resid = fluxes - zero_point[visit_id][:, None] * tile_ref
    return coadd, zero_point, flux_resid
```

```python
import jax
import jax.numpy as jnp
from jax import lax
from jax.experimental import pallas as pl
from jax.experimental.pallas import tpu as pltpu
from jax.sharding import PartitionSpec as P

F32 = jnp.float32
BF16 = jnp.bfloat16
S = 512
NP = 16
NV = 8
TD = 8
MESH = pl.DeviceIdType.MESH

ORDER = ("x0", "y0", "z0", "x1", "y1", "z1")
ROWS = (48, 48, 48, 48, 32, 32)
OFFS = (0, 48, 96, 144, 192, 224)
PIECES = (
    ((0, 0, 48, 0),),
    ((0, 48, 16, 0), (1, 0, 32, 16)),
    ((1, 32, 32, 0), (2, 0, 16, 32)),
    ((2, 16, 48, 0),),
    ((3, 0, 32, 0),),
    ((3, 32, 32, 0),),
)


def gray(c):
    return c // 2, (c // 2 + c % 2) % 2


def nt(a, b):
    return lax.dot_general(a, b, (((1,), (1,)), ((), ())), preferred_element_type=F32)


def tn(a, b):
    return lax.dot_general(a, b, (((0,), (0,)), ((), ())), preferred_element_type=F32)


def nn(a, b):
    return jnp.dot(a, b, preferred_element_type=F32)


def split(a):
    high = a.astype(BF16)
    return high, (a - high.astype(F32)).astype(BF16)


def profile(center, first, count):
    pixel = lax.broadcasted_iota(jnp.int32, (count, S), 0).astype(F32) + first
    distance = pixel - center
    return jnp.exp(distance * distance * (-1.0 / 12.5)).astype(BF16)


def kernel(
    patch_sm, weight_sm, warped_hbm, mr_hbm, mc_hbm, srow_ref, scol_ref,
    coadd_ref, zp_ref, resid_ref,
    warped, mr, mc, acc, rc, r0, r1, r2, fin, r3, r4, r5,
    metag, fluxg, pg, refg, sg, colt, rowt, bth, btl, at, mch, mcl, mrow, sblk,
    tab_i, tab_w, lsem, csem_s, csem_r, rsem_s, rsem_r, gsem_s, gsem_r, vsem_s, vsem_r, asem_s, asem_r,
):
    v = lax.axis_index("visit")
    me = lax.axis_index("patch")
    x, core = v // 2, v % 2
    y, z = me // 4, me % 4
    side = {}
    for name, c in (("x", x), ("y", y), ("z", z)):
        side[name + "1"], side[name + "0"] = gray(c)
    flip0 = lambda c: c + 1 - 2 * (c % 2)
    partner = {
        "x0": (flip0(x) * 2 + core, me), "x1": ((3 - x) * 2 + core, me),
        "y0": (v, flip0(y) * 4 + z), "y1": (v, (3 - y) * 4 + z),
        "z0": (v, y * 4 + flip0(z)), "z1": (v, y * 4 + 3 - z),
    }
    other = 1 - core
    mate = (x * 2 + other, me)

    def remote(src, dst, ss, rs, where):
        return pltpu.make_async_remote_copy(
            src_ref=src, dst_ref=dst, send_sem=ss, recv_sem=rs,
            device_id={"visit": where[0], "patch": where[1]}, device_id_type=MESH,
        )

    barrier = pltpu.get_barrier_semaphore()

    @pl.loop(1, NP)
    def _(o):
        pl.semaphore_signal(barrier, inc=1, device_id={"visit": v, "patch": (me + o) % NP}, device_id_type=MESH)

    @pl.loop(1, NV)
    def _(o):
        pl.semaphore_signal(barrier, inc=1, device_id={"visit": (v + o) % NV, "patch": me}, device_id_type=MESH)

    load_w = pltpu.make_async_copy(warped_hbm, warped, lsem.at[0])
    load_w.start()
    load_r = pltpu.make_async_copy(mr_hbm, mr, lsem.at[1])
    load_r.start()
    load_c = pltpu.make_async_copy(mc_hbm, mc, lsem.at[2])
    load_c.start()

    @pl.loop(0, NP)
    def _(p):
        ia = jnp.int32(0)
        ib = jnp.int32(0)
        wa = jnp.float32(0)
        wb = jnp.float32(0)
        seen = jnp.int32(0)
        for t in range(TD):
            hit = (patch_sm[t] == p).astype(jnp.int32)
            first = hit * (1 - jnp.minimum(seen, 1))
            second = hit * (seen == 1).astype(jnp.int32)
            ia = ia + first * t
            ib = ib + second * t
            wa = wa + first.astype(F32) * weight_sm[t]
            wb = wb + second.astype(F32) * weight_sm[t]
            seen = seen + hit
        tab_i[p] = ia
        tab_i[NP + p] = ib
        tab_w[p] = wa
        tab_w[NP + p] = wb

    for t in range(TD):
        metag[me, t : t + 1, :] = jnp.full((1, 128), patch_sm[t].astype(F32), F32)
        metag[me, TD + t : TD + t + 1, :] = jnp.full((1, 128), weight_sm[t], F32)
    for c in range(4):
        metag[me, 16 + c : 17 + c, :] = srow_ref[:, c * 128 : (c + 1) * 128].astype(F32)
        metag[me, 20 + c : 21 + c, :] = scol_ref[:, c * 128 : (c + 1) * 128].astype(F32)

    pl.semaphore_wait(barrier, NP - 1 + NV - 1)

    def gather_copy(buf, kind, o):
        return remote(buf.at[me], buf.at[me], gsem_s.at[kind, o], gsem_r.at[kind, o], (v, (me + o) % NP))

    def gather_start(buf, kind):
        @pl.loop(1, NP)
        def _(o):
            gather_copy(buf, kind, o).start()

    def gather_wait(buf, kind):
        @pl.loop(1, NP)
        def _(o):
            theirs = (me - o + NP) % NP
            remote(buf.at[theirs], buf.at[theirs], gsem_s.at[kind, o], gsem_r.at[kind, o], (v, (me + o) % NP)).wait()

    gather_start(metag, 0)

    def combine(h):
        @pl.loop(0, NP)
        def _(p):
            ia, ib = tab_i[p], tab_i[NP + p]
            wa = jnp.full((16, 128), tab_w[p], F32).astype(BF16)
            wb = jnp.full((16, 128), tab_w[NP + p], F32).astype(BF16)
            bits = {}
            bits["y1"], bits["y0"] = gray(p // 4)
            bits["z1"], bits["z0"] = gray(p % 4)
            for xr in range(4):
                bits["x1"], bits["x0"] = gray(xr)
                for k in range(6):
                    place = 0
                    for j in range(6):
                        place = place * 2 + bits[ORDER[(k + j) % 6]]
                    for tile, first, count, to in PIECES[k]:
                        for i in range(0, count, 16):
                            rows = pl.ds(pl.multiple_of((xr * 2 + h) * 64 + first + i, 16), 16)
                            lanes = slice(tile * 128, tile * 128 + 128)
                            acc[h, place, OFFS[k] + to + i : OFFS[k] + to + i + 16, :] = (
                                warped[ia, rows, lanes] * wa + warped[ib, rows, lanes] * wb
                            )

    load_w.wait()
    combine(other)

    def core_copy(k):
        rows = pl.ds(OFFS[k], ROWS[k])
        return remote(acc.at[other, :, rows, :], rc.at[:, rows, :], csem_s.at[k], csem_r.at[k], mate)

    for k in range(6):
        core_copy(k).start()
    combine(core)
    gather_wait(metag, 0)

    def source_lines(q, first):
        return jnp.concatenate([metag[q, first + c : first + c + 1, :] for c in range(4)], axis=1)

    def measure(first, last):
        @pl.loop(first, last)
        def _(t):
            q = patch_sm[t]
            row_of = source_lines(q, 16)
            col_of = source_lines(q, 20)

            @pl.loop(0, 4)
            def _(b):
                start = pl.multiple_of(b * 128, 128)
                colt[pl.ds(start, 128), :] = profile(col_of, (b * 128).astype(F32), 128)

            def part(b, total):
                start = pl.multiple_of(b * 128, 128)
                by_col = nn(warped[t, pl.ds(start, 128), :], colt[...])
                rows = profile(row_of, (b * 128).astype(F32), 128).astype(F32)
                return total + jnp.sum((by_col * rows).reshape(16, 8, S), axis=0)

            total = lax.fori_loop(0, 4, part, jnp.zeros((8, S), F32))
            fluxg[me, pl.ds(t, 1), :] = jnp.sum(total, axis=0, keepdims=True)

    bufs = (r0, r1, r2, r3, r4, r5)

    def base_of(k, j):
        lo = 0 if j < 3 else 3
        base = 0
        for i in range(lo, j):
            base = base + side[ORDER[(k + i) % 6]] * (32 >> i)
        return base

    def round_copy(k, j):
        d = ORDER[(k + j) % 6]
        half = 32 >> j
        start = base_of(k, j) + (1 - side[d]) * half
        rows = pl.ds(OFFS[k], ROWS[k])
        src = acc.at[core, pl.ds(start, half), rows, :] if j < 3 else fin.at[pl.ds(start, half), rows, :]
        return remote(src, bufs[j].at[:, rows, :], rsem_s.at[j, k], rsem_r.at[j, k], partner[d])

    def round_add(k, j):
        half = 32 >> j
        keep = base_of(k, j + 1) if j != 2 else base_of(k, 2) + side[ORDER[(k + 2) % 6]] * half
        rows = pl.ds(OFFS[k], ROWS[k])
        step = min(half, 8)

        @pl.loop(0, half // step)
        def _(i):
            new = bufs[j][pl.ds(i * step, step), rows, :]
            at_ = pl.ds(keep + i * step, step)
            if j < 2:
                acc[core, at_, rows, :] = acc[core, at_, rows, :] + new
            elif j == 2:
                fin[pl.ds(i * step, step), rows, :] = acc[core, at_, rows, :].astype(F32) + new.astype(F32)
            else:
                fin[at_, rows, :] = fin[at_, rows, :] + new

    def core_add(k):
        rows = pl.ds(OFFS[k], ROWS[k])

        @pl.loop(0, 8)
        def _(i):
            at_ = pl.ds(i * 8, 8)
            acc[core, at_, rows, :] = acc[core, at_, rows, :] + rc[at_, rows, :]

    measure(0, 2)
    for k in range(6):
        core_copy(k).wait()
        core_add(k)
        round_copy(k, 0).start()
    measure(2, 6)
    for k in range(6):
        round_copy(k, 0).wait()
        round_add(k, 0)
        round_copy(k, 1).start()
    measure(6, 8)
    gather_start(fluxg, 1)
    for k in range(6):
        round_copy(k, 1).wait()
        round_add(k, 1)
        round_copy(k, 2).start()

    own_row = source_lines(me, 16)
    own_col = source_lines(me, 20)

    @pl.loop(0, 4)
    def _(b):
        start = pl.multiple_of(b * 128, 128)
        colt[pl.ds(start, 128), :] = profile(own_col, (b * 128).astype(F32), 128)
        rowt[pl.ds(start, 128), :] = profile(own_row, (b * 128).astype(F32), 128)

    load_r.wait()
    load_c.wait()

    @pl.loop(0, 4)
    def _(b):
        start = pl.multiple_of(b * 128, 128)
        cols = pl.ds(start, 128)
        high, low = split(mc[:, cols])
        value = tn(high, colt[...]) + tn(low, colt[...])
        high, low = split(value)
        bth[cols, :] = high
        btl[cols, :] = low
        high, low = split(mr[:, cols])
        at[cols, :] = tn(high, rowt[...]) + tn(low, rowt[...])
        high, low = split(mc[cols, :])
        mch[cols, :] = high
        mcl[cols, :] = low

    for j in range(2, 5):
        for k in range(6):
            round_copy(k, j).wait()
            round_add(k, j)
            round_copy(k, j + 1).start()
    for k in range(6):
        round_copy(k, 5).wait()
        place = base_of(k, 6)
        for tile, first, count, to in PIECES[k]:
            here = slice(OFFS[k] + to, OFFS[k] + to + count)
            sblk[first : first + count, tile * 128 : tile * 128 + 128] = fin[place, here, :] + r5[0, here, :]

    own = pl.ds(pl.multiple_of(v * 64, 64), 64)
    sg[own, :] = sblk[...].astype(BF16)

    def rows_of(who):
        return pl.ds(pl.multiple_of(who * 64, 64), 64)

    def share_copy(o):
        if o == 0:
            return remote(sg.at[own, :], sg.at[own, :], asem_s.at[0], asem_r.at[0], mate)
        return remote(sg.at[own, :], sg.at[own, :], asem_s.at[o], asem_r.at[o], (((x + o) % 4) * 2 + core, me))

    def pass_copy(o):
        rows = rows_of(((x - o + 4) % 4) * 2 + core)
        return remote(sg.at[rows, :], sg.at[rows, :], asem_s.at[3 + o], asem_r.at[3 + o], mate)

    high, low = split(sblk[...])
    value = nn(high, bth[...]) + nn(low, bth[...]) + nn(high, btl[...])
    partial = jnp.sum(value * at[own, :], axis=0, keepdims=True)
    for c in range(4):
        pg[v, c : c + 1, :] = partial[:, c * 128 : (c + 1) * 128]
    mine = metag[:, 0:8, :].reshape(128, 128) == me.astype(F32)
    weights = jnp.where(mine, metag[:, 8:16, :].reshape(128, 128), 0.0)
    pg[v, 4:5, :] = jnp.sum(weights, axis=0, keepdims=True)
    pg[v, 5:8, :] = jnp.zeros((3, 128), F32)

    @pl.loop(1, NV)
    def _(o):
        remote(pg.at[v], pg.at[v], vsem_s.at[o], vsem_r.at[o], ((v + o) % NV, me)).start()

    for o in (1, 3, 2, 0):
        share_copy(o).start()

    gather_wait(fluxg, 1)
    tile = lax.broadcasted_iota(jnp.int32, (128, 128), 0)
    lane = lax.broadcasted_iota(jnp.int32, (128, 128), 1)
    hits = (metag[:, 0:8, :].reshape(128, 128) == (lane % 16).astype(F32)) & (tile % 4 == lane // 16)
    hits = jnp.where(hits, 1.0, 0.0).astype(BF16)
    high, low = split(fluxg[...].reshape(128, S))
    sums = tn(hits, high) + tn(hits, low)
    counts = tn(hits, jnp.ones((128, 128), BF16))

    @pl.loop(1, NV)
    def _(o):
        theirs = (v - o + NV) % NV
        remote(pg.at[theirs], pg.at[theirs], vsem_s.at[o], vsem_r.at[o], ((v + o) % NV, me)).wait()

    total = jnp.sum(pg[...], axis=0)
    inverse = 1.0 / total[4:5, :]
    refg[me] = total * inverse
    gather_start(refg, 2)

    for o in (1, 3, 2):
        rows = rows_of(((x - o + 4) % 4) * 2 + core)
        remote(sg.at[rows, :], sg.at[rows, :], asem_s.at[o], asem_r.at[o], (((x + o) % 4) * 2 + core, me)).wait()
        pass_copy(o).start()
    mates = rows_of(x * 2 + other)
    remote(sg.at[mates, :], sg.at[mates, :], asem_s.at[0], asem_r.at[0], mate).wait()
    for o in (1, 3, 2):
        rows = rows_of(((x - o + 4) % 4) * 2 + other)
        remote(sg.at[rows, :], sg.at[rows, :], asem_s.at[3 + o], asem_r.at[3 + o], mate).wait()
    high, low = split(mr[own, :])
    matched = nn(high, sg[...]) + nn(low, sg[...])
    high, low = split(matched)
    matched = nt(high, mch[...]) + nt(low, mch[...]) + nt(high, mcl[...])
    for c in range(4):
        coadd_ref[:, c * 128 : (c + 1) * 128] = matched[:, c * 128 : (c + 1) * 128] * inverse

    gather_wait(refg, 2)
    refs = jnp.concatenate([refg[:, c, :] for c in range(4)], axis=1)
    squares = jnp.sum(refs * refs, axis=1, keepdims=True)
    fits = []
    for u in range(4):
        rows = slice(u * 16, u * 16 + 16)
        top = jnp.sum(jnp.sum(sums[rows, :] * refs, axis=0, keepdims=True), axis=1, keepdims=True)
        low = jnp.sum(counts[rows, 0:1] * squares, axis=0, keepdims=True)
        fits.append(top / low)
    for u in range(4):
        zp_ref[u : u + 1, :] = jnp.broadcast_to(fits[u], (1, 128))
    for t in range(TD):
        q = patch_sm[t]
        template = jnp.concatenate([refg[q, c : c + 1, :] for c in range(4)], axis=1)
        resid_ref[t : t + 1, :] = fluxg[me, t : t + 1, :] - fits[t % 4] * template


def fused(tile_patch, tile_weight, warped, match_rows, match_cols, src_row, src_col):
    dma = pltpu.SemaphoreType.DMA
    any_ = pl.BlockSpec(memory_space=pl.ANY)
    smem = pl.BlockSpec(memory_space=pltpu.SMEM)
    vmem = pl.BlockSpec(memory_space=pltpu.VMEM)
    return pl.pallas_call(
        kernel,
        out_shape=(
            jax.ShapeDtypeStruct((64, S), F32),
            jax.ShapeDtypeStruct((4, 128), F32),
            jax.ShapeDtypeStruct((TD, S), F32),
        ),
        in_specs=[smem, smem, any_, any_, any_, vmem, vmem],
        out_specs=(vmem, vmem, vmem),
        scratch_shapes=[
            pltpu.VMEM((TD, S, S), BF16),
            pltpu.VMEM((S, S), F32),
            pltpu.VMEM((S, S), F32),
            pltpu.VMEM((2, 64, 256, 128), BF16),
            pltpu.VMEM((64, 256, 128), BF16),
            pltpu.VMEM((32, 256, 128), BF16),
            pltpu.VMEM((16, 256, 128), BF16),
            pltpu.VMEM((8, 256, 128), BF16),
            pltpu.VMEM((8, 256, 128), F32),
            pltpu.VMEM((4, 256, 128), F32),
            pltpu.VMEM((2, 256, 128), F32),
            pltpu.VMEM((1, 256, 128), F32),
            pltpu.VMEM((NP, 24, 128), F32),
            pltpu.VMEM((NP, TD, S), F32),
            pltpu.VMEM((NV, 8, 128), F32),
            pltpu.VMEM((NP, 8, 128), F32),
            pltpu.VMEM((S, S), BF16),
            pltpu.VMEM((S, S), BF16),
            pltpu.VMEM((S, S), BF16),
            pltpu.VMEM((S, S), BF16),
            pltpu.VMEM((S, S), BF16),
            pltpu.VMEM((S, S), F32),
            pltpu.VMEM((S, S), BF16),
            pltpu.VMEM((S, S), BF16),
            pltpu.VMEM((64, S), F32),
            pltpu.VMEM((64, S), F32),
            pltpu.SMEM((2 * NP,), jnp.int32),
            pltpu.SMEM((2 * NP,), F32),
            dma((3,)), dma((6,)), dma((6,)), dma((6, 6)), dma((6, 6)),
            dma((3, NP)), dma((3, NP)), dma((NV,)), dma((NV,)), dma((8,)), dma((8,)),
        ],
        compiler_params=pltpu.CompilerParams(
            collective_id=0, has_side_effects=True, vmem_limit_bytes=60 * 1024 * 1024
        ),
        name="coadd",
    )(tile_patch, tile_weight, warped, match_rows, match_cols, src_row, src_col)


def shards(
    images, warp_rows, warp_cols, tile_weight, tile_patch, match_rows, match_cols, src_row, src_col
):
    half_warp = jnp.einsum(
        "tij,tkj->tik", images, warp_cols, preferred_element_type=jnp.float32
    ).astype(jnp.bfloat16)
    warped = jnp.einsum(
        "tij,tjk->tik", warp_rows, half_warp, preferred_element_type=jnp.float32
    ).astype(jnp.bfloat16)
    coadd, zero_point, resid = fused(
        tile_patch, tile_weight.astype(F32), warped, match_rows[0], match_cols[0], src_row, src_col
    )
    return coadd[None], zero_point[:, 0], resid


def solution(mesh):
    in_specs = (
        P(("visit", "patch"), None, None),
        P(("visit", "patch"), None, None),
        P(("visit", "patch"), None, None),
        P(("visit", "patch")),
        P(("visit", "patch")),
        P("patch", None, None),
        P("patch", None, None),
        P("patch", None),
        P("patch", None),
    )
    out_specs = (P("patch", "visit", None), P("visit"), P(("visit", "patch"), None))
    return jax.shard_map(shards, mesh=mesh, in_specs=in_specs, out_specs=out_specs, check_vma=False)
```

```python
import jax
import jax.numpy as jnp
from jax import lax
from jax.experimental import pallas as pl
from jax.experimental.pallas import tpu as pltpu
from jax.sharding import PartitionSpec as P

F32 = jnp.float32
BF16 = jnp.bfloat16
S = 512
NP = 16
NV = 8
TD = 8
MESH = pl.DeviceIdType.MESH

ORDER = ("x0", "y0", "z0", "x1", "y1", "z1")
ROWS = ((32, 32, 16, 16, 16, 16), (16, 16, 32, 32, 16, 16))
OFFS = tuple(
    tuple(s * 128 + sum(ROWS[s][:k]) for k in range(6)) for s in range(2)
)


def gray(c):
    return c // 2, (c // 2 + c % 2) % 2


def nt(a, b):
    return lax.dot_general(a, b, (((1,), (1,)), ((), ())), preferred_element_type=F32)


def tn(a, b):
    return lax.dot_general(a, b, (((0,), (0,)), ((), ())), preferred_element_type=F32)


def nn(a, b):
    return jnp.dot(a, b, preferred_element_type=F32)


def split(a):
    high = a.astype(BF16)
    return high, (a - high.astype(F32)).astype(BF16)


def profile(center, first, count):
    pixel = lax.broadcasted_iota(jnp.int32, (count, S), 0).astype(F32) + first
    distance = pixel - center
    return jnp.exp(distance * distance * (-1.0 / 12.5)).astype(BF16)


def kernel(
    patch_sm, weight_ref, img_hbm, wr_hbm, wc_hbm, mr_hbm, mc_hbm, srow_ref, scol_ref,
    coadd_ref, zp_ref, resid_ref,
    img, wr, wc, halfs, warped, mr, mc, acc, rc, r0, r1, r2, fin, r3, r4, r5,
    metag, fluxg, pg, refg, sg, colt, rowt, bth, btl, at, mch, mcl, mrow, sblk,
    tab_i, tab_w, weight_sm, tsem, lsem, csem_s, csem_r, rsem_s, rsem_r, gsem_s, gsem_r, vsem_s, vsem_r, asem_s, asem_r,
):
    v = lax.axis_index("visit")
    me = lax.axis_index("patch")
    x, core = v // 2, v % 2
    y, z = me // 4, me % 4
    side = {}
    for name, c in (("x", x), ("y", y), ("z", z)):
        side[name + "1"], side[name + "0"] = gray(c)
    flip0 = lambda c: c + 1 - 2 * (c % 2)
    partner = {
        "x0": (flip0(x) * 2 + core, me), "x1": ((3 - x) * 2 + core, me),
        "y0": (v, flip0(y) * 4 + z), "y1": (v, (3 - y) * 4 + z),
        "z0": (v, y * 4 + flip0(z)), "z1": (v, y * 4 + 3 - z),
    }
    other = 1 - core
    mate = (x * 2 + other, me)

    def remote(src, dst, ss, rs, where):
        return pltpu.make_async_remote_copy(
            src_ref=src, dst_ref=dst, send_sem=ss, recv_sem=rs,
            device_id={"visit": where[0], "patch": where[1]}, device_id_type=MESH,
        )

    barrier = pltpu.get_barrier_semaphore()

    @pl.loop(1, NP)
    def _(o):
        pl.semaphore_signal(barrier, inc=1, device_id={"visit": v, "patch": (me + o) % NP}, device_id_type=MESH)

    @pl.loop(1, NV)
    def _(o):
        pl.semaphore_signal(barrier, inc=1, device_id={"visit": (v + o) % NV, "patch": me}, device_id_type=MESH)

    def tile_load(i, t):
        hbm, buf = ((wc_hbm, wc), (img_hbm, img), (wr_hbm, wr))[i]
        return pltpu.make_async_copy(hbm.at[t], buf.at[t], tsem.at[i, t])

    @pl.loop(0, TD)
    def _(t):
        for i in range(3):
            tile_load(i, t).start()

    load_r = pltpu.make_async_copy(mr_hbm, mr, lsem.at[1])
    load_r.start()
    load_c = pltpu.make_async_copy(mc_hbm, mc, lsem.at[2])
    load_c.start()

    lane8 = lax.broadcasted_iota(jnp.int32, (1, TD), 1)
    for t in range(TD):
        weight_sm[t] = jnp.sum(jnp.where(lane8 == t, weight_ref[...].astype(F32), 0.0))

    @pl.loop(0, NP)
    def _(p):
        ia = jnp.int32(0)
        ib = jnp.int32(0)
        wa = jnp.float32(0)
        wb = jnp.float32(0)
        seen = jnp.int32(0)
        for t in range(TD):
            hit = (patch_sm[t] == p).astype(jnp.int32)
            first = hit * (1 - jnp.minimum(seen, 1))
            second = hit * (seen == 1).astype(jnp.int32)
            ia = ia + first * t
            ib = ib + second * t
            wa = wa + first.astype(F32) * weight_sm[t]
            wb = wb + second.astype(F32) * weight_sm[t]
            seen = seen + hit
        tab_i[p] = ia
        tab_i[NP + p] = ib
        tab_w[p] = wa
        tab_w[NP + p] = wb

    for t in range(TD):
        metag[me, t : t + 1, :] = jnp.full((1, 128), patch_sm[t].astype(F32), F32)
        metag[me, TD + t : TD + t + 1, :] = jnp.full((1, 128), weight_sm[t], F32)
    for c in range(4):
        metag[me, 16 + c : 17 + c, :] = srow_ref[:, c * 128 : (c + 1) * 128].astype(F32)
        metag[me, 20 + c : 21 + c, :] = scol_ref[:, c * 128 : (c + 1) * 128].astype(F32)

    def gather_copy(buf, kind, o):
        return remote(buf.at[me], buf.at[me], gsem_s.at[kind, o], gsem_r.at[kind, o], (v, (me + o) % NP))

    def gather_start(buf, kind):
        @pl.loop(1, NP)
        def _(o):
            gather_copy(buf, kind, o).start()

    def gather_wait(buf, kind):
        @pl.loop(1, NP)
        def _(o):
            theirs = (me - o + NP) % NP
            remote(buf.at[theirs], buf.at[theirs], gsem_s.at[kind, o], gsem_r.at[kind, o], (v, (me + o) % NP)).wait()

    def warp(first, last, s):
        cols = slice(s * 256, s * 256 + 256)

        @pl.loop(first // 2, last // 2)
        def _(tt):
            for i in range(2):
                t = tt * 2 + i
                if s == 0:
                    for n in range(3):
                        tile_load(n, t).wait()
                halfs[i] = nt(img[t], wc[t, cols, :]).astype(BF16)
            for i in range(2):
                t = tt * 2 + i
                warped[t, :, cols] = nn(wr[t], halfs[i]).astype(BF16)

    def combine(h, s):
        @pl.loop(0, NP)
        def _(p):
            ia, ib = tab_i[p], tab_i[NP + p]
            wa = jnp.full((16, 128), tab_w[p], F32).astype(BF16)
            wb = jnp.full((16, 128), tab_w[NP + p], F32).astype(BF16)
            bits = {}
            bits["y1"], bits["y0"] = gray(p // 4)
            bits["z1"], bits["z0"] = gray(p % 4)
            for xr in range(4):
                bits["x1"], bits["x0"] = gray(xr)
                for k in range(6):
                    place = 0
                    for j in range(6):
                        place = place * 2 + bits[ORDER[(k + j) % 6]]
                    for at_ in range(OFFS[s][k], OFFS[s][k] + ROWS[s][k], 16):
                        rows = pl.ds(pl.multiple_of((xr * 2 + h) * 64 + at_ % 64, 16), 16)
                        lanes = slice(at_ // 64 * 128, at_ // 64 * 128 + 128)
                        acc[h, place, at_ : at_ + 16, :] = (
                            warped[ia, rows, lanes] * wa + warped[ib, rows, lanes] * wb
                        )

    def core_copy(s, k):
        rows = pl.ds(OFFS[s][k], ROWS[s][k])
        return remote(acc.at[other, :, rows, :], rc.at[:, rows, :], csem_s.at[s, k], csem_r.at[s, k], mate)

    def core_start(s):
        for k in range(6):
            core_copy(s, k).start()

    def source_lines(q, first):
        return jnp.concatenate([metag[q, first + c : first + c + 1, :] for c in range(4)], axis=1)

    def measure(first, last):
        @pl.loop(first, last)
        def _(t):
            q = patch_sm[t]
            row_of = source_lines(q, 16)
            col_of = source_lines(q, 20)

            @pl.loop(0, 4)
            def _(b):
                start = pl.multiple_of(b * 128, 128)
                colt[pl.ds(start, 128), :] = profile(col_of, (b * 128).astype(F32), 128)

            def part(b, total):
                start = pl.multiple_of(b * 128, 128)
                by_col = nn(warped[t, pl.ds(start, 128), :], colt[...])
                rows = profile(row_of, (b * 128).astype(F32), 128).astype(F32)
                return total + jnp.sum((by_col * rows).reshape(16, 8, S), axis=0)

            total = lax.fori_loop(0, 4, part, jnp.zeros((8, S), F32))
            fluxg[me, pl.ds(t, 1), :] = jnp.sum(total, axis=0, keepdims=True)

    bufs = (r0, r1, r2, r3, r4, r5)

    def base_of(k, j):
        lo = 0 if j < 3 else 3
        base = 0
        for i in range(lo, j):
            base = base + side[ORDER[(k + i) % 6]] * (32 >> i)
        return base

    def round_copy(s, k, j):
        d = ORDER[(k + j) % 6]
        half = 32 >> j
        start = base_of(k, j) + (1 - side[d]) * half
        rows = pl.ds(OFFS[s][k], ROWS[s][k])
        src = acc.at[core, pl.ds(start, half), rows, :] if j < 3 else fin.at[pl.ds(start, half), rows, :]
        return remote(src, bufs[j].at[:, rows, :], rsem_s.at[j, s * 6 + k], rsem_r.at[j, s * 6 + k], partner[d])

    def round_add(s, k, j):
        half = 32 >> j
        keep = base_of(k, j + 1) if j != 2 else base_of(k, 2) + side[ORDER[(k + 2) % 6]] * half
        rows = pl.ds(OFFS[s][k], ROWS[s][k])
        step = min(half, 8)

        @pl.loop(0, half // step)
        def _(i):
            new = bufs[j][pl.ds(i * step, step), rows, :]
            at_ = pl.ds(keep + i * step, step)
            if j < 2:
                acc[core, at_, rows, :] = acc[core, at_, rows, :] + new
            elif j == 2:
                fin[pl.ds(i * step, step), rows, :] = acc[core, at_, rows, :].astype(F32) + new.astype(F32)
            else:
                fin[at_, rows, :] = fin[at_, rows, :] + new

    def core_add(s):
        for k in range(6):
            rows = pl.ds(OFFS[s][k], ROWS[s][k])
            core_copy(s, k).wait()

            @pl.loop(0, 4)
            def _(i):
                at_ = pl.ds(i * 16, 16)
                acc[core, at_, rows, :] = acc[core, at_, rows, :] + rc[at_, rows, :]

            round_copy(s, k, 0).start()

    def advance(s, j):
        for k in range(6):
            round_copy(s, k, j).wait()
            round_add(s, k, j)
            round_copy(s, k, j + 1).start()

    def finish(s):
        for k in range(6):
            round_copy(s, k, 5).wait()
            place = base_of(k, 6)
            for at_ in range(OFFS[s][k], OFFS[s][k] + ROWS[s][k], 16):
                here = slice(at_, at_ + 16)
                lanes = slice(at_ // 64 * 128, at_ // 64 * 128 + 128)
                sblk[at_ % 64 : at_ % 64 + 16, lanes] = fin[place, here, :] + r5[0, here, :]

    warp(0, TD, 0)
    pl.semaphore_wait(barrier, NP - 1 + NV - 1)
    combine(other, 0)
    core_start(0)
    gather_start(metag, 0)
    combine(core, 0)
    warp(0, 4, 1)
    core_add(0)
    warp(4, TD, 1)
    combine(other, 1)
    core_start(1)
    combine(core, 1)
    gather_wait(metag, 0)
    measure(0, 1)
    core_add(1)
    advance(0, 0)
    measure(1, 3)
    advance(1, 0)
    advance(0, 1)
    measure(3, 6)
    advance(1, 1)
    advance(0, 2)
    measure(6, 8)
    gather_start(fluxg, 1)
    advance(1, 2)
    advance(0, 3)

    own_row = source_lines(me, 16)
    own_col = source_lines(me, 20)

    @pl.loop(0, 4)
    def _(b):
        start = pl.multiple_of(b * 128, 128)
        colt[pl.ds(start, 128), :] = profile(own_col, (b * 128).astype(F32), 128)
        rowt[pl.ds(start, 128), :] = profile(own_row, (b * 128).astype(F32), 128)

    load_r.wait()
    load_c.wait()

    @pl.loop(0, 4)
    def _(b):
        start = pl.multiple_of(b * 128, 128)
        cols = pl.ds(start, 128)
        high, low = split(mc[:, cols])
        value = tn(high, colt[...]) + tn(low, colt[...])
        high, low = split(value)
        bth[cols, :] = high
        btl[cols, :] = low
        high, low = split(mr[:, cols])
        at[cols, :] = tn(high, rowt[...]) + tn(low, rowt[...])
        high, low = split(mc[cols, :])
        mch[cols, :] = high
        mcl[cols, :] = low

    advance(1, 3)
    advance(0, 4)
    advance(1, 4)
    finish(0)
    finish(1)

    own = pl.ds(pl.multiple_of(v * 64, 64), 64)
    sg[own, :] = sblk[...].astype(BF16)

    def rows_of(who):
        return pl.ds(pl.multiple_of(who * 64, 64), 64)

    def share_copy(o):
        if o == 0:
            return remote(sg.at[own, :], sg.at[own, :], asem_s.at[0], asem_r.at[0], mate)
        return remote(sg.at[own, :], sg.at[own, :], asem_s.at[o], asem_r.at[o], (((x + o) % 4) * 2 + core, me))

    def pass_copy(o):
        rows = rows_of(((x - o + 4) % 4) * 2 + core)
        return remote(sg.at[rows, :], sg.at[rows, :], asem_s.at[3 + o], asem_r.at[3 + o], mate)

    high, low = split(sblk[...])
    value = nn(high, bth[...]) + nn(low, bth[...]) + nn(high, btl[...])
    partial = jnp.sum(value * at[own, :], axis=0, keepdims=True)
    for c in range(4):
        pg[v, c : c + 1, :] = partial[:, c * 128 : (c + 1) * 128]
    mine = metag[:, 0:8, :].reshape(128, 128) == me.astype(F32)
    weights = jnp.where(mine, metag[:, 8:16, :].reshape(128, 128), 0.0)
    pg[v, 4:5, :] = jnp.sum(weights, axis=0, keepdims=True)
    pg[v, 5:8, :] = jnp.zeros((3, 128), F32)

    @pl.loop(1, NV)
    def _(o):
        remote(pg.at[v], pg.at[v], vsem_s.at[o], vsem_r.at[o], ((v + o) % NV, me)).start()

    for o in (1, 3, 2, 0):
        share_copy(o).start()

    gather_wait(fluxg, 1)
    tile = lax.broadcasted_iota(jnp.int32, (128, 128), 0)
    lane = lax.broadcasted_iota(jnp.int32, (128, 128), 1)
    hits = (metag[:, 0:8, :].reshape(128, 128) == (lane % 16).astype(F32)) & (tile % 4 == lane // 16)
    hits = jnp.where(hits, 1.0, 0.0).astype(BF16)
    high, low = split(fluxg[...].reshape(128, S))
    sums = tn(hits, high) + tn(hits, low)
    counts = tn(hits, jnp.ones((128, 128), BF16))

    @pl.loop(1, NV)
    def _(o):
        theirs = (v - o + NV) % NV
        remote(pg.at[theirs], pg.at[theirs], vsem_s.at[o], vsem_r.at[o], ((v + o) % NV, me)).wait()

    total = jnp.sum(pg[...], axis=0)
    inverse = 1.0 / total[4:5, :]
    refg[me] = total * inverse
    gather_start(refg, 2)

    for o in (1, 3, 2):
        rows = rows_of(((x - o + 4) % 4) * 2 + core)
        remote(sg.at[rows, :], sg.at[rows, :], asem_s.at[o], asem_r.at[o], (((x + o) % 4) * 2 + core, me)).wait()
        pass_copy(o).start()
    mates = rows_of(x * 2 + other)
    remote(sg.at[mates, :], sg.at[mates, :], asem_s.at[0], asem_r.at[0], mate).wait()
    for o in (1, 3, 2):
        rows = rows_of(((x - o + 4) % 4) * 2 + other)
        remote(sg.at[rows, :], sg.at[rows, :], asem_s.at[3 + o], asem_r.at[3 + o], mate).wait()
    high, low = split(mr[own, :])
    matched = nn(high, sg[...]) + nn(low, sg[...])
    high, low = split(matched)
    matched = nt(high, mch[...]) + nt(low, mch[...]) + nt(high, mcl[...])
    for c in range(4):
        coadd_ref[:, c * 128 : (c + 1) * 128] = matched[:, c * 128 : (c + 1) * 128] * inverse

    gather_wait(refg, 2)
    refs = jnp.concatenate([refg[:, c, :] for c in range(4)], axis=1)
    squares = jnp.sum(refs * refs, axis=1, keepdims=True)
    fits = []
    for u in range(4):
        rows = slice(u * 16, u * 16 + 16)
        top = jnp.sum(jnp.sum(sums[rows, :] * refs, axis=0, keepdims=True), axis=1, keepdims=True)
        low = jnp.sum(counts[rows, 0:1] * squares, axis=0, keepdims=True)
        fits.append(top / low)
    for u in range(4):
        zp_ref[u : u + 1, :] = jnp.broadcast_to(fits[u], (1, 128))
    for t in range(TD):
        q = patch_sm[t]
        template = jnp.concatenate([refg[q, c : c + 1, :] for c in range(4)], axis=1)
        resid_ref[t : t + 1, :] = fluxg[me, t : t + 1, :] - fits[t % 4] * template


def fused(tile_patch, tile_weight, images, warp_rows, warp_cols, match_rows, match_cols, src_row, src_col):
    dma = pltpu.SemaphoreType.DMA
    any_ = pl.BlockSpec(memory_space=pl.ANY)
    smem = pl.BlockSpec(memory_space=pltpu.SMEM)
    vmem = pl.BlockSpec(memory_space=pltpu.VMEM)
    return pl.pallas_call(
        kernel,
        out_shape=(
            jax.ShapeDtypeStruct((64, S), F32),
            jax.ShapeDtypeStruct((4, 128), F32),
            jax.ShapeDtypeStruct((TD, S), F32),
        ),
        in_specs=[smem, vmem, any_, any_, any_, any_, any_, vmem, vmem],
        out_specs=(vmem, vmem, vmem),
        scratch_shapes=[
            pltpu.VMEM((TD, S, S), BF16),
            pltpu.VMEM((TD, S, S), BF16),
            pltpu.VMEM((TD, S, S), BF16),
            pltpu.VMEM((2, S, 256), BF16),
            pltpu.VMEM((TD, S, S), BF16),
            pltpu.VMEM((S, S), F32),
            pltpu.VMEM((S, S), F32),
            pltpu.VMEM((2, 64, 256, 128), BF16),
            pltpu.VMEM((64, 256, 128), BF16),
            pltpu.VMEM((32, 256, 128), BF16),
            pltpu.VMEM((16, 256, 128), BF16),
            pltpu.VMEM((8, 256, 128), BF16),
            pltpu.VMEM((8, 256, 128), F32),
            pltpu.VMEM((4, 256, 128), F32),
            pltpu.VMEM((2, 256, 128), F32),
            pltpu.VMEM((1, 256, 128), F32),
            pltpu.VMEM((NP, 24, 128), F32),
            pltpu.VMEM((NP, TD, S), F32),
            pltpu.VMEM((NV, 8, 128), F32),
            pltpu.VMEM((NP, 8, 128), F32),
            pltpu.VMEM((S, S), BF16),
            pltpu.VMEM((S, S), BF16),
            pltpu.VMEM((S, S), BF16),
            pltpu.VMEM((S, S), BF16),
            pltpu.VMEM((S, S), BF16),
            pltpu.VMEM((S, S), F32),
            pltpu.VMEM((S, S), BF16),
            pltpu.VMEM((S, S), BF16),
            pltpu.VMEM((64, S), F32),
            pltpu.VMEM((64, S), F32),
            pltpu.SMEM((2 * NP,), jnp.int32),
            pltpu.SMEM((2 * NP,), F32),
            pltpu.SMEM((TD,), F32),
            dma((3, TD)), dma((3,)), dma((2, 6)), dma((2, 6)), dma((6, 12)), dma((6, 12)),
            dma((3, NP)), dma((3, NP)), dma((NV,)), dma((NV,)), dma((8,)), dma((8,)),
        ],
        compiler_params=pltpu.CompilerParams(
            collective_id=0, has_side_effects=True, vmem_limit_bytes=60 * 1024 * 1024
        ),
        name="coadd",
    )(tile_patch, tile_weight, images, warp_rows, warp_cols, match_rows, match_cols, src_row, src_col)


def shards(
    images, warp_rows, warp_cols, tile_weight, tile_patch, match_rows, match_cols, src_row, src_col
):
    coadd, zero_point, resid = fused(
        tile_patch, tile_weight[None], images, warp_rows, warp_cols, match_rows[0], match_cols[0], src_row, src_col
    )
    return coadd[None], zero_point[:, 0], resid


def solution(mesh):
    in_specs = (
        P(("visit", "patch"), None, None),
        P(("visit", "patch"), None, None),
        P(("visit", "patch"), None, None),
        P(("visit", "patch")),
        P(("visit", "patch")),
        P("patch", None, None),
        P("patch", None, None),
        P("patch", None),
        P("patch", None),
    )
    out_specs = (P("patch", "visit", None), P("visit"), P(("visit", "patch"), None))
    return jax.shard_map(shards, mesh=mesh, in_specs=in_specs, out_specs=out_specs, check_vma=False)
```

```python
import jax
import jax.numpy as jnp
from jax import lax
from jax.experimental import pallas as pl
from jax.experimental.pallas import tpu as pltpu
from jax.sharding import PartitionSpec as P

F32 = jnp.float32
BF16 = jnp.bfloat16
S = 512
NP = 16
NV = 8
TD = 8
MESH = pl.DeviceIdType.MESH

ORDER = ("x0", "y0", "z0", "x1", "y1", "z1")
UNITS = (((0, 1), (2, 3), (4,), (5,), (6,), (7,)), ((8,), (9,), (10, 11), (12, 13), (14,), (15,)))


def gray(c):
    return c // 2, (c // 2 + c % 2) % 2


def nt(a, b):
    return lax.dot_general(a, b, (((1,), (1,)), ((), ())), preferred_element_type=F32)


def tn(a, b):
    return lax.dot_general(a, b, (((0,), (0,)), ((), ())), preferred_element_type=F32)


def nn(a, b):
    return jnp.dot(a, b, preferred_element_type=F32)


def split(a):
    high = a.astype(BF16)
    return high, (a - high.astype(F32)).astype(BF16)


def profile(center, first, count):
    pixel = lax.broadcasted_iota(jnp.int32, (count, S), 0).astype(F32) + first
    distance = pixel - center
    return jnp.exp(distance * distance * (-1.0 / 12.5)).astype(BF16)


def kernel(
    patch_sm, weight_ref, img_hbm, wr_hbm, wc_hbm, mr_hbm, mc_hbm, srow_ref, scol_ref,
    coadd_ref, zp_ref, resid_ref,
    img, wr, wc, halfs, warped, mr, mc, acc, rc, r0, r1, r2, fin,
    metag, infog, fluxg, fluxo, pg, refg, sg, colt, rowt, bth, at, mch, mcl, sblk,
    tab_i, tab_w, weight_sm, tsem, lsem, csem_s, csem_r, rsem_s, rsem_r, fsem_s, fsem_r, gsem_s, gsem_r, vsem_s, vsem_r, asem_s, asem_r,
):
    v = lax.axis_index("visit")
    me = lax.axis_index("patch")
    x, core = v // 2, v % 2
    y, z = me // 4, me % 4
    side = {}
    for name, c in (("x", x), ("y", y), ("z", z)):
        side[name + "1"], side[name + "0"] = gray(c)
    flip0 = lambda c: c + 1 - 2 * (c % 2)
    partner = {
        "x0": (flip0(x) * 2 + core, me), "x1": ((3 - x) * 2 + core, me),
        "y0": (v, flip0(y) * 4 + z), "y1": (v, (3 - y) * 4 + z),
        "z0": (v, y * 4 + flip0(z)), "z1": (v, y * 4 + 3 - z),
    }
    other = 1 - core
    mate = (x * 2 + other, me)

    def remote(src, dst, ss, rs, where):
        return pltpu.make_async_remote_copy(
            src_ref=src, dst_ref=dst, send_sem=ss, recv_sem=rs,
            device_id={"visit": where[0], "patch": where[1]}, device_id_type=MESH,
        )

    barrier = pltpu.get_barrier_semaphore()

    @pl.loop(1, NP)
    def _(o):
        pl.semaphore_signal(barrier, inc=1, device_id={"visit": v, "patch": (me + o) % NP}, device_id_type=MESH)

    @pl.loop(1, NV)
    def _(o):
        pl.semaphore_signal(barrier, inc=1, device_id={"visit": (v + o) % NV, "patch": me}, device_id_type=MESH)

    flips = {"x": (flip0(x), 3 - x), "y": (flip0(y), 3 - y), "z": (flip0(z), 3 - z)}
    met = set()
    for k in range(6):
        last = tuple(sorted(ORDER[(k + 3 + i) % 6] for i in range(3)))
        met |= {last, last[:2], (last[0], last[2])}
    for dims in sorted(met):
        where = {"x": x, "y": y, "z": z}
        for d in dims:
            where[d[0]] = flips[d[0]][int(d[1])]
        there = {"visit": where["x"] * 2 + core, "patch": where["y"] * 4 + where["z"]}
        pl.semaphore_signal(barrier, inc=1, device_id=there, device_id_type=MESH)
    peers = NP - 1 + NV - 1 + len(met)

    def tile_load(i, t):
        hbm, buf = ((wc_hbm, wc), (img_hbm, img), (wr_hbm, wr))[i]
        return pltpu.make_async_copy(hbm.at[t], buf.at[t], tsem.at[i, t])

    @pl.loop(0, TD)
    def _(t):
        for i in range(3):
            tile_load(i, t).start()

    load_r = pltpu.make_async_copy(mr_hbm, mr, lsem.at[1])
    load_r.start()
    load_c = pltpu.make_async_copy(mc_hbm, mc, lsem.at[2])
    load_c.start()

    lane8 = lax.broadcasted_iota(jnp.int32, (1, TD), 1)
    for t in range(TD):
        weight_sm[t] = jnp.sum(jnp.where(lane8 == t, weight_ref[...].astype(F32), 0.0))

    @pl.loop(0, NP)
    def _(p):
        ia = jnp.int32(0)
        ib = jnp.int32(0)
        wa = jnp.float32(0)
        wb = jnp.float32(0)
        seen = jnp.int32(0)
        for t in range(TD):
            hit = (patch_sm[t] == p).astype(jnp.int32)
            first = hit * (1 - jnp.minimum(seen, 1))
            second = hit * (seen == 1).astype(jnp.int32)
            ia = ia + first * t
            ib = ib + second * t
            wa = wa + first.astype(F32) * weight_sm[t]
            wb = wb + second.astype(F32) * weight_sm[t]
            seen = seen + hit
        tab_i[p] = ia
        tab_i[NP + p] = ib
        tab_w[p] = wa
        tab_w[NP + p] = wb

    low_lanes = lax.broadcasted_iota(jnp.int32, (1, 128), 1) < 64
    for t in range(TD):
        infog[me, t : t + 1, :] = jnp.where(low_lanes, patch_sm[t].astype(F32), weight_sm[t])
    for c in range(4):
        metag[me, c : 1 + c, :] = srow_ref[:, c * 128 : (c + 1) * 128].astype(F32)
        metag[me, 4 + c : 5 + c, :] = scol_ref[:, c * 128 : (c + 1) * 128].astype(F32)

    def gather_copy(buf, kind, o):
        return remote(buf.at[me], buf.at[me], gsem_s.at[kind, o], gsem_r.at[kind, o], (v, (me + o) % NP))

    def gather_start(buf, kind):
        @pl.loop(1, NP)
        def _(o):
            gather_copy(buf, kind, o).start()

    def gather_wait(buf, kind):
        @pl.loop(1, NP)
        def _(o):
            theirs = (me - o + NP) % NP
            remote(buf.at[theirs], buf.at[theirs], gsem_s.at[kind, o], gsem_r.at[kind, o], (v, (me + o) % NP)).wait()

    def warp(first, last, step):
        @pl.loop(first // step, last // step)
        def _(tt):
            for i in range(step):
                t = tt * step + i
                for n in range(2):
                    tile_load(n, t).wait()
                halfs[i] = nt(img[t], wc[t]).astype(BF16)
            for i in range(step):
                t = tt * step + i
                tile_load(2, t).wait()
                warped[t] = nn(wr[t], halfs[i]).astype(BF16)

    def combine(h, s):
        @pl.loop(0, NP)
        def _(p):
            ia, ib = tab_i[p], tab_i[NP + p]
            wa = jnp.full((16, 128), tab_w[p], F32).astype(BF16)
            wb = jnp.full((16, 128), tab_w[NP + p], F32).astype(BF16)
            bits = {}
            bits["y1"], bits["y0"] = gray(p // 4)
            bits["z1"], bits["z0"] = gray(p % 4)
            for xr in range(4):
                bits["x1"], bits["x0"] = gray(xr)
                for k in range(6):
                    place = 0
                    for j in range(6):
                        place = place * 2 + bits[ORDER[(k + j) % 6]]
                    for i, unit in enumerate(UNITS[s][k]):
                        rows = pl.ds(pl.multiple_of((xr * 2 + h) * 64 + unit % 4 * 16, 16), 16)
                        lanes = slice(unit // 4 * 128, unit // 4 * 128 + 128)
                        acc[h, UNITS[s][k][0] * 64 + place * len(UNITS[s][k]) + i] = (
                            warped[ia, rows, lanes] * wa + warped[ib, rows, lanes] * wb
                        )

    def part(s, k, total, start, count):
        n = len(UNITS[s][k])
        return pl.ds(UNITS[s][k][0] * total + start * n, count * n)

    def core_copy(s, k):
        span = part(s, k, 64, 0, 64)
        return remote(acc.at[other, span], rc.at[span], csem_s.at[s, k], csem_r.at[s, k], mate)

    def core_start(s):
        for k in range(6):
            core_copy(s, k).start()

    def source_lines(q, first):
        return jnp.concatenate([metag[q, first + c : first + c + 1, :] for c in range(4)], axis=1)

    def measure(first, last):
        @pl.loop(first, last)
        def _(t):
            q = patch_sm[t]
            row_of = source_lines(q, 0)
            col_of = source_lines(q, 4)

            @pl.loop(0, 4)
            def _(b):
                start = pl.multiple_of(b * 128, 128)
                colt[pl.ds(start, 128), :] = profile(col_of, (b * 128).astype(F32), 128)

            def part(b, total):
                start = pl.multiple_of(b * 128, 128)
                by_col = nn(warped[t, pl.ds(start, 128), :], colt[...])
                rows = profile(row_of, (b * 128).astype(F32), 128).astype(F32)
                return total + jnp.sum((by_col * rows).reshape(16, 8, S), axis=0)

            total = lax.fori_loop(0, 4, part, jnp.zeros((8, S), F32))
            fluxo[pl.ds(t, 1), :] = jnp.sum(total, axis=0, keepdims=True)

    bufs = (r0, r1, r2)

    def base_of(k, j):
        base = 0
        for i in range(j):
            base = base + side[ORDER[(k + i) % 6]] * (32 >> i)
        return base

    def round_copy(s, k, j):
        d = ORDER[(k + j) % 6]
        half = 32 >> j
        start = base_of(k, j) + (1 - side[d]) * half
        src = acc.at[core, part(s, k, 64, start, half)]
        dst = bufs[j].at[part(s, k, half, 0, half)]
        return remote(src, dst, rsem_s.at[j, s * 6 + k], rsem_r.at[j, s * 6 + k], partner[d])

    def round_add(s, k, j):
        half = 32 >> j
        step = min(half, 16)

        @pl.loop(0, half // step)
        def _(i):
            at_ = part(s, k, 64, base_of(k, j + 1) + i * step, step)
            acc[core, at_] = acc[core, at_] + bufs[j][part(s, k, half, i * step, step)]

    def last_copy(s, k, e):
        place = base_of(k, 3)
        where = {"x": x, "y": y, "z": z}
        for i in range(3):
            d = ORDER[(k + 3 + i) % 6]
            bit = side[d]
            if e >> (2 - i) & 1:
                bit = 1 - bit
                c = where[d[0]]
                where[d[0]] = flip0(c) if d[1] == "0" else 3 - c
            place = place + bit * (4 >> i)
        there = (where["x"] * 2 + core, where["y"] * 4 + where["z"])
        return remote(
            acc.at[core, part(s, k, 64, place, 1)], fin.at[part(s, k, 8, e, 1)],
            fsem_s.at[s * 6 + k, e], fsem_r.at[s * 6 + k, e], there,
        )

    def core_add(s):
        for k in range(6):
            core_copy(s, k).wait()

            @pl.loop(0, 4)
            def _(i):
                at_ = part(s, k, 64, i * 16, 16)
                acc[core, at_] = acc[core, at_] + rc[at_]

            round_copy(s, k, 0).start()

    def advance(s, j):
        for k in range(6):
            round_copy(s, k, j).wait()
            round_add(s, k, j)
            if j < 2:
                round_copy(s, k, j + 1).start()
            else:
                for e in (7, 6, 5, 3, 4, 2, 1):
                    last_copy(s, k, e).start()

    def finish(s):
        for k in range(6):
            n = len(UNITS[s][k])
            place = base_of(k, 6)
            for e in (1, 2, 4, 3, 5, 6, 7):
                last_copy(s, k, e).wait()
            for i, unit in enumerate(UNITS[s][k]):
                value = acc[core, UNITS[s][k][0] * 64 + place * n + i].astype(F32)
                for e in range(1, 8):
                    value = value + fin[UNITS[s][k][0] * 8 + e * n + i].astype(F32)
                lanes = slice(unit // 4 * 128, unit // 4 * 128 + 128)
                sblk[unit % 4 * 16 : unit % 4 * 16 + 16, lanes] = value

    warp(0, 6, 2)
    warp(6, TD, 1)
    pl.semaphore_wait(barrier, peers)
    combine(other, 0)
    core_start(0)
    gather_start(metag, 0)
    combine(other, 1)
    core_start(1)
    combine(core, 0)
    combine(core, 1)
    core_add(0)
    core_add(1)
    gather_wait(metag, 0)
    measure(0, 2)
    advance(0, 0)
    measure(2, 4)
    advance(1, 0)
    measure(4, 6)
    advance(0, 1)
    advance(1, 1)
    measure(6, 8)
    fluxg[me] = fluxo[...].astype(BF16)
    advance(0, 2)
    gather_start(infog, 3)

    own_row = source_lines(me, 0)
    own_col = source_lines(me, 4)

    @pl.loop(0, 4)
    def _(b):
        start = pl.multiple_of(b * 128, 128)
        colt[pl.ds(start, 128), :] = profile(own_col, (b * 128).astype(F32), 128)
        rowt[pl.ds(start, 128), :] = profile(own_row, (b * 128).astype(F32), 128)

    load_r.wait()
    load_c.wait()

    @pl.loop(0, 4)
    def _(b):
        start = pl.multiple_of(b * 128, 128)
        cols = pl.ds(start, 128)
        high, low = split(mc[:, cols])
        value = tn(high, colt[...]) + tn(low, colt[...])
        bth[cols, :] = value.astype(BF16)
        high, low = split(mr[:, cols])
        at[cols, :] = tn(high, rowt[...]) + tn(low, rowt[...])
        high, low = split(mc[cols, :])
        mch[cols, :] = high
        mcl[cols, :] = low

    advance(1, 2)
    gather_start(fluxg, 1)
    gather_wait(infog, 3)
    info = infog[...].reshape(128, 128)
    mine = (info == me.astype(F32)) & (lax.broadcasted_iota(jnp.int32, (128, 128), 1) < 64)
    weights = jnp.where(mine, pltpu.roll(info, 64, 1), 0.0)
    weight_sum = jnp.sum(jnp.sum(weights, axis=0, keepdims=True), axis=1, keepdims=True) * (1.0 / 64.0)
    finish(0)
    finish(1)

    own = pl.ds(pl.multiple_of(v * 64, 64), 64)
    sg[own, :] = sblk[...].astype(BF16)

    def rows_of(who):
        return pl.ds(pl.multiple_of(who * 64, 64), 64)

    def share_copy(o):
        if o == 0:
            return remote(sg.at[own, :], sg.at[own, :], asem_s.at[0], asem_r.at[0], mate)
        return remote(sg.at[own, :], sg.at[own, :], asem_s.at[o], asem_r.at[o], (((x + o) % 4) * 2 + core, me))

    def pass_copy(o):
        rows = rows_of(((x - o + 4) % 4) * 2 + core)
        return remote(sg.at[rows, :], sg.at[rows, :], asem_s.at[3 + o], asem_r.at[3 + o], mate)

    high, low = split(sblk[...])
    value = nn(jnp.concatenate([high, low], axis=0), bth[...])
    value = value[0:64] + value[64:128]
    partial = jnp.sum(value * at[own, :], axis=0, keepdims=True)
    for c in range(4):
        pg[v, c : c + 1, :] = partial[:, c * 128 : (c + 1) * 128]
    pg[v, 4:5, :] = jnp.broadcast_to(weight_sum, (1, 128))
    pg[v, 5:8, :] = jnp.zeros((3, 128), F32)

    @pl.loop(1, NV)
    def _(o):
        remote(pg.at[v], pg.at[v], vsem_s.at[o], vsem_r.at[o], ((v + o) % NV, me)).start()

    for o in (1, 3, 2, 0):
        share_copy(o).start()

    gather_wait(fluxg, 1)
    tile = lax.broadcasted_iota(jnp.int32, (128, 128), 0)
    lane = lax.broadcasted_iota(jnp.int32, (128, 128), 1)
    hits = (infog[...].reshape(128, 128) == (lane % 16).astype(F32)) & (tile % 4 == lane // 16)
    hits = jnp.where(hits, 1.0, 0.0).astype(BF16)
    sums = tn(hits, fluxg[...].reshape(128, S))
    counts = tn(hits, jnp.ones((128, 128), BF16))

    @pl.loop(1, NV)
    def _(o):
        theirs = (v - o + NV) % NV
        remote(pg.at[theirs], pg.at[theirs], vsem_s.at[o], vsem_r.at[o], ((v + o) % NV, me)).wait()

    total = jnp.sum(pg[...], axis=0)
    inverse = 1.0 / total[4:5, :]
    refg[me] = total * inverse
    gather_start(refg, 2)

    for o in (1, 3, 2):
        rows = rows_of(((x - o + 4) % 4) * 2 + core)
        remote(sg.at[rows, :], sg.at[rows, :], asem_s.at[o], asem_r.at[o], (((x + o) % 4) * 2 + core, me)).wait()
        pass_copy(o).start()
    mates = rows_of(x * 2 + other)
    remote(sg.at[mates, :], sg.at[mates, :], asem_s.at[0], asem_r.at[0], mate).wait()
    for o in (1, 3, 2):
        rows = rows_of(((x - o + 4) % 4) * 2 + other)
        remote(sg.at[rows, :], sg.at[rows, :], asem_s.at[3 + o], asem_r.at[3 + o], mate).wait()
    high, low = split(mr[own, :])
    matched = nn(high, sg[...]) + nn(low, sg[...])
    high, low = split(matched)
    matched = nt(high, mch[...]) + nt(low, mch[...]) + nt(high, mcl[...])
    for c in range(4):
        coadd_ref[:, c * 128 : (c + 1) * 128] = matched[:, c * 128 : (c + 1) * 128] * inverse

    gather_wait(refg, 2)
    refs = jnp.concatenate([refg[:, c, :] for c in range(4)], axis=1)
    squares = jnp.sum(refs * refs, axis=1, keepdims=True)
    fits = []
    for u in range(4):
        rows = slice(u * 16, u * 16 + 16)
        top = jnp.sum(jnp.sum(sums[rows, :] * refs, axis=0, keepdims=True), axis=1, keepdims=True)
        low = jnp.sum(counts[rows, 0:1] * squares, axis=0, keepdims=True)
        fits.append(top / low)
    for u in range(4):
        zp_ref[u : u + 1, :] = jnp.broadcast_to(fits[u], (1, 128))
    for t in range(TD):
        q = patch_sm[t]
        template = jnp.concatenate([refg[q, c : c + 1, :] for c in range(4)], axis=1)
        resid_ref[t : t + 1, :] = fluxo[t : t + 1, :] - fits[t % 4] * template


def fused(tile_patch, tile_weight, images, warp_rows, warp_cols, match_rows, match_cols, src_row, src_col):
    dma = pltpu.SemaphoreType.DMA
    any_ = pl.BlockSpec(memory_space=pl.ANY)
    smem = pl.BlockSpec(memory_space=pltpu.SMEM)
    vmem = pl.BlockSpec(memory_space=pltpu.VMEM)
    return pl.pallas_call(
        kernel,
        out_shape=(
            jax.ShapeDtypeStruct((64, S), F32),
            jax.ShapeDtypeStruct((4, 128), F32),
            jax.ShapeDtypeStruct((TD, S), F32),
        ),
        in_specs=[smem, vmem, any_, any_, any_, any_, any_, vmem, vmem],
        out_specs=(vmem, vmem, vmem),
        scratch_shapes=[
            pltpu.VMEM((TD, S, S), BF16),
            pltpu.VMEM((TD, S, S), BF16),
            pltpu.VMEM((TD, S, S), BF16),
            pltpu.VMEM((2, S, S), BF16),
            pltpu.VMEM((TD, S, S), BF16),
            pltpu.VMEM((S, S), F32),
            pltpu.VMEM((S, S), F32),
            pltpu.VMEM((2, 64 * 16, 16, 128), BF16),
            pltpu.VMEM((64 * 16, 16, 128), BF16),
            pltpu.VMEM((32 * 16, 16, 128), BF16),
            pltpu.VMEM((16 * 16, 16, 128), BF16),
            pltpu.VMEM((8 * 16, 16, 128), BF16),
            pltpu.VMEM((8 * 16, 16, 128), BF16),
            pltpu.VMEM((NP, 8, 128), F32),
            pltpu.VMEM((NP, TD, 128), F32),
            pltpu.VMEM((NP, TD, S), BF16),
            pltpu.VMEM((TD, S), F32),
            pltpu.VMEM((NV, 8, 128), F32),
            pltpu.VMEM((NP, 8, 128), F32),
            pltpu.VMEM((S, S), BF16),
            pltpu.VMEM((S, S), BF16),
            pltpu.VMEM((S, S), BF16),
            pltpu.VMEM((S, S), BF16),
            pltpu.VMEM((S, S), F32),
            pltpu.VMEM((S, S), BF16),
            pltpu.VMEM((S, S), BF16),
            pltpu.VMEM((64, S), F32),
            pltpu.SMEM((2 * NP,), jnp.int32),
            pltpu.SMEM((2 * NP,), F32),
            pltpu.SMEM((TD,), F32),
            dma((3, TD)), dma((3,)), dma((2, 6)), dma((2, 6)), dma((3, 12)), dma((3, 12)), dma((12, 8)), dma((12, 8)),
            dma((4, NP)), dma((4, NP)), dma((NV,)), dma((NV,)), dma((8,)), dma((8,)),
        ],
        compiler_params=pltpu.CompilerParams(
            collective_id=0, has_side_effects=True, vmem_limit_bytes=60 * 1024 * 1024
        ),
        name="coadd",
    )(tile_patch, tile_weight, images, warp_rows, warp_cols, match_rows, match_cols, src_row, src_col)


def store(coadd_in, zp_in, resid_in, coadd_ref, zp_ref, resid_ref):
    coadd_ref[0] = coadd_in[...]
    resid_ref[...] = resid_in[...]
    for u in range(4):
        zp_ref[u] = jnp.max(zp_in[u : u + 1, :])


def shards(
    images, warp_rows, warp_cols, tile_weight, tile_patch, match_rows, match_cols, src_row, src_col
):
    coadd, zero_point, resid = fused(
        tile_patch, tile_weight[None], images, warp_rows, warp_cols, match_rows[0], match_cols[0], src_row, src_col
    )
    vmem = pl.BlockSpec(memory_space=pltpu.VMEM)
    return pl.pallas_call(
        store,
        out_shape=(
            jax.ShapeDtypeStruct((1, 64, S), F32),
            jax.ShapeDtypeStruct((4,), F32),
            jax.ShapeDtypeStruct((TD, S), F32),
        ),
        in_specs=[vmem, vmem, vmem],
        out_specs=(vmem, pl.BlockSpec(memory_space=pltpu.SMEM), vmem),
        name="store",
    )(coadd, zero_point, resid)


def solution(mesh):
    in_specs = (
        P(("visit", "patch"), None, None),
        P(("visit", "patch"), None, None),
        P(("visit", "patch"), None, None),
        P(("visit", "patch")),
        P(("visit", "patch")),
        P("patch", None, None),
        P("patch", None, None),
        P("patch", None),
        P("patch", None),
    )
    out_specs = (P("patch", "visit", None), P("visit"), P(("visit", "patch"), None))
    return jax.shard_map(shards, mesh=mesh, in_specs=in_specs, out_specs=out_specs, check_vma=False)
```

```python
import jax
import jax.numpy as jnp
from jax import lax
from jax.experimental import pallas as pl
from jax.experimental.pallas import tpu as pltpu
from jax.sharding import PartitionSpec as P

F32 = jnp.float32
BF16 = jnp.bfloat16
S = 512
NP = 16
NV = 8
TD = 8
MESH = pl.DeviceIdType.MESH

ORDER = ("x0", "y0", "z0", "x1", "y1", "z1")
UNITS = (((0, 1), (2, 3), (4,), (5,), (6,), (7,)), ((8,), (9,), (10, 11), (12, 13), (14,), (15,)))


def gray(c):
    return c // 2, (c // 2 + c % 2) % 2


def nt(a, b):
    return lax.dot_general(a, b, (((1,), (1,)), ((), ())), preferred_element_type=F32)


def tn(a, b):
    return lax.dot_general(a, b, (((0,), (0,)), ((), ())), preferred_element_type=F32)


def nn(a, b):
    return jnp.dot(a, b, preferred_element_type=F32)


def split(a):
    high = a.astype(BF16)
    return high, (a - high.astype(F32)).astype(BF16)


def profile(center, first, count):
    pixel = lax.broadcasted_iota(jnp.int32, (count, S), 0).astype(F32) + first
    distance = pixel - center
    return jnp.exp(distance * distance * (-1.0 / 12.5)).astype(BF16)


def kernel(
    patch_sm, weight_ref, img_hbm, wr_hbm, wc_hbm, mr_hbm, mc_hbm, srow_ref, scol_ref,
    coadd_ref, zp_ref, resid_ref,
    img, wr, wc, halfs, warped, mr, mc, acc, rc, r0, r1, r2, fin, sums, counts, value,
    metag, infog, fluxg, fluxo, pg, refg, sg, colt, rowt, bth, at, mch, mcl, sblk,
    tab_i, tab_w, weight_sm, tsem, lsem, csem_s, csem_r, rsem_s, rsem_r, fsem_s, fsem_r, gsem_s, gsem_r, vsem_s, vsem_r, asem_s, asem_r,
):
    v = lax.axis_index("visit")
    me = lax.axis_index("patch")
    x, core = v // 2, v % 2
    y, z = me // 4, me % 4
    side = {}
    for name, c in (("x", x), ("y", y), ("z", z)):
        side[name + "1"], side[name + "0"] = gray(c)
    flip0 = lambda c: c + 1 - 2 * (c % 2)
    partner = {
        "x0": (flip0(x) * 2 + core, me), "x1": ((3 - x) * 2 + core, me),
        "y0": (v, flip0(y) * 4 + z), "y1": (v, (3 - y) * 4 + z),
        "z0": (v, y * 4 + flip0(z)), "z1": (v, y * 4 + 3 - z),
    }
    other = 1 - core
    mate = (x * 2 + other, me)

    def remote(src, dst, ss, rs, where):
        return pltpu.make_async_remote_copy(
            src_ref=src, dst_ref=dst, send_sem=ss, recv_sem=rs,
            device_id={"visit": where[0], "patch": where[1]}, device_id_type=MESH,
        )

    barrier = pltpu.get_barrier_semaphore()

    @pl.loop(1, NP)
    def _(o):
        pl.semaphore_signal(barrier, inc=1, device_id={"visit": v, "patch": (me + o) % NP}, device_id_type=MESH)

    @pl.loop(1, NV)
    def _(o):
        pl.semaphore_signal(barrier, inc=1, device_id={"visit": (v + o) % NV, "patch": me}, device_id_type=MESH)

    flips = {"x": (flip0(x), 3 - x), "y": (flip0(y), 3 - y), "z": (flip0(z), 3 - z)}
    met = set()
    for k in range(6):
        last = tuple(sorted(ORDER[(k + 3 + i) % 6] for i in range(3)))
        met |= {last, last[:2], (last[0], last[2])}
    for dims in sorted(met):
        where = {"x": x, "y": y, "z": z}
        for d in dims:
            where[d[0]] = flips[d[0]][int(d[1])]
        there = {"visit": where["x"] * 2 + core, "patch": where["y"] * 4 + where["z"]}
        pl.semaphore_signal(barrier, inc=1, device_id=there, device_id_type=MESH)
    peers = NP - 1 + NV - 1 + len(met)

    def tile_load(i, t):
        hbm, buf = ((wc_hbm, wc), (img_hbm, img), (wr_hbm, wr))[i]
        return pltpu.make_async_copy(hbm.at[t], buf.at[t], tsem.at[i, t])

    @pl.loop(0, TD)
    def _(t):
        for i in range(3):
            tile_load(i, t).start()

    load_r = pltpu.make_async_copy(mr_hbm, mr, lsem.at[1])
    load_c = pltpu.make_async_copy(mc_hbm, mc, lsem.at[2])

    lane8 = lax.broadcasted_iota(jnp.int32, (1, TD), 1)
    for t in range(TD):
        weight_sm[t] = jnp.sum(jnp.where(lane8 == t, weight_ref[...].astype(F32), 0.0))

    @pl.loop(0, NP)
    def _(p):
        ia = jnp.int32(0)
        ib = jnp.int32(0)
        wa = jnp.float32(0)
        wb = jnp.float32(0)
        seen = jnp.int32(0)
        for t in range(TD):
            hit = (patch_sm[t] == p).astype(jnp.int32)
            first = hit * (1 - jnp.minimum(seen, 1))
            second = hit * (seen == 1).astype(jnp.int32)
            ia = ia + first * t
            ib = ib + second * t
            wa = wa + first.astype(F32) * weight_sm[t]
            wb = wb + second.astype(F32) * weight_sm[t]
            seen = seen + hit
        tab_i[p] = ia
        tab_i[NP + p] = ib
        tab_w[p] = wa
        tab_w[NP + p] = wb

    low_lanes = lax.broadcasted_iota(jnp.int32, (1, 128), 1) < 64
    for t in range(TD):
        infog[me, t : t + 1, :] = jnp.where(low_lanes, patch_sm[t].astype(F32), weight_sm[t])
    for c in range(4):
        metag[me, c : 1 + c, :] = srow_ref[:, c * 128 : (c + 1) * 128].astype(F32)
        metag[me, 4 + c : 5 + c, :] = scol_ref[:, c * 128 : (c + 1) * 128].astype(F32)

    def gather_copy(buf, kind, o):
        return remote(buf.at[me], buf.at[me], gsem_s.at[kind, o], gsem_r.at[kind, o], (v, (me + o) % NP))

    def gather_start(buf, kind):
        @pl.loop(1, NP)
        def _(o):
            gather_copy(buf, kind, o).start()

    def gather_wait(buf, kind):
        @pl.loop(1, NP)
        def _(o):
            theirs = (me - o + NP) % NP
            remote(buf.at[theirs], buf.at[theirs], gsem_s.at[kind, o], gsem_r.at[kind, o], (v, (me + o) % NP)).wait()

    def warp(first, last, step):
        @pl.loop(first // step, last // step)
        def _(tt):
            for i in range(step):
                t = tt * step + i
                for n in range(2):
                    tile_load(n, t).wait()
                halfs[i] = nt(img[t], wc[t]).astype(BF16)
            for i in range(step):
                t = tt * step + i
                tile_load(2, t).wait()
                warped[t] = nn(wr[t], halfs[i]).astype(BF16)

    def combine(h, s):
        @pl.loop(0, NP)
        def _(p):
            ia, ib = tab_i[p], tab_i[NP + p]
            wa = jnp.full((16, 128), tab_w[p], F32).astype(BF16)
            wb = jnp.full((16, 128), tab_w[NP + p], F32).astype(BF16)
            bits = {}
            bits["y1"], bits["y0"] = gray(p // 4)
            bits["z1"], bits["z0"] = gray(p % 4)
            for xr in range(4):
                bits["x1"], bits["x0"] = gray(xr)
                for k in range(6):
                    place = 0
                    for j in range(6):
                        place = place * 2 + bits[ORDER[(k + j) % 6]]
                    for i, unit in enumerate(UNITS[s][k]):
                        rows = pl.ds(pl.multiple_of((xr * 2 + h) * 64 + unit % 4 * 16, 16), 16)
                        lanes = slice(unit // 4 * 128, unit // 4 * 128 + 128)
                        acc[h, UNITS[s][k][0] * 64 + place * len(UNITS[s][k]) + i] = (
                            warped[ia, rows, lanes] * wa + warped[ib, rows, lanes] * wb
                        )

    def part(s, k, total, start, count):
        n = len(UNITS[s][k])
        return pl.ds(UNITS[s][k][0] * total + start * n, count * n)

    def core_copy(s, k):
        span = part(s, k, 64, 0, 64)
        return remote(acc.at[other, span], rc.at[span], csem_s.at[s, k], csem_r.at[s, k], mate)

    def core_start(s):
        for k in range(6):
            core_copy(s, k).start()

    def source_lines(q, first):
        return jnp.concatenate([metag[q, first + c : first + c + 1, :] for c in range(4)], axis=1)

    def measure(first, last):
        @pl.loop(first, last)
        def _(t):
            q = patch_sm[t]
            row_of = source_lines(q, 0)
            col_of = source_lines(q, 4)

            @pl.loop(0, 4)
            def _(b):
                start = pl.multiple_of(b * 128, 128)
                colt[pl.ds(start, 128), :] = profile(col_of, (b * 128).astype(F32), 128)

            def part(b, total):
                start = pl.multiple_of(b * 128, 128)
                by_col = nn(warped[t, pl.ds(start, 128), :], colt[...])
                rows = profile(row_of, (b * 128).astype(F32), 128).astype(F32)
                return total + jnp.sum((by_col * rows).reshape(16, 8, S), axis=0)

            total = lax.fori_loop(0, 4, part, jnp.zeros((8, S), F32))
            fluxo[pl.ds(t, 1), :] = jnp.sum(total, axis=0, keepdims=True)

    bufs = (r0, r1, r2)

    def base_of(k, j):
        base = 0
        for i in range(j):
            base = base + side[ORDER[(k + i) % 6]] * (32 >> i)
        return base

    def round_copy(s, k, j):
        d = ORDER[(k + j) % 6]
        half = 32 >> j
        start = base_of(k, j) + (1 - side[d]) * half
        src = acc.at[core, part(s, k, 64, start, half)]
        dst = bufs[j].at[part(s, k, half, 0, half)]
        return remote(src, dst, rsem_s.at[j, s * 6 + k], rsem_r.at[j, s * 6 + k], partner[d])

    def round_add(s, k, j):
        half = 32 >> j
        step = min(half, 16)

        @pl.loop(0, half // step)
        def _(i):
            at_ = part(s, k, 64, base_of(k, j + 1) + i * step, step)
            acc[core, at_] = acc[core, at_] + bufs[j][part(s, k, half, i * step, step)]

    def last_copy(s, k, e):
        place = base_of(k, 3)
        where = {"x": x, "y": y, "z": z}
        for i in range(3):
            d = ORDER[(k + 3 + i) % 6]
            bit = side[d]
            if e >> (2 - i) & 1:
                bit = 1 - bit
                c = where[d[0]]
                where[d[0]] = flip0(c) if d[1] == "0" else 3 - c
            place = place + bit * (4 >> i)
        there = (where["x"] * 2 + core, where["y"] * 4 + where["z"])
        return remote(
            acc.at[core, part(s, k, 64, place, 1)], fin.at[part(s, k, 8, e, 1)],
            fsem_s.at[s * 6 + k, e], fsem_r.at[s * 6 + k, e], there,
        )

    def core_add(s):
        for k in range(6):
            core_copy(s, k).wait()

            @pl.loop(0, 4)
            def _(i):
                at_ = part(s, k, 64, i * 16, 16)
                acc[core, at_] = acc[core, at_] + rc[at_]

            round_copy(s, k, 0).start()

    def advance(s, j):
        for k in range(6):
            round_copy(s, k, j).wait()
            round_add(s, k, j)
            if j < 2:
                round_copy(s, k, j + 1).start()
            else:
                for e in (7, 6, 5, 3, 4, 2, 1):
                    last_copy(s, k, e).start()

    def finish(s):
        for k in range(6):
            n = len(UNITS[s][k])
            place = base_of(k, 6)
            for e in (1, 2, 4, 3, 5, 6, 7):
                last_copy(s, k, e).wait()
            for i, unit in enumerate(UNITS[s][k]):
                value = acc[core, UNITS[s][k][0] * 64 + place * n + i].astype(F32)
                for e in range(1, 8):
                    value = value + fin[UNITS[s][k][0] * 8 + e * n + i].astype(F32)
                lanes = slice(unit // 4 * 128, unit // 4 * 128 + 128)
                sblk[unit % 4 * 16 : unit % 4 * 16 + 16, lanes] = value

    def tables():
        own_row = source_lines(me, 0)
        own_col = source_lines(me, 4)

        @pl.loop(0, 4)
        def _(b):
            start = pl.multiple_of(b * 128, 128)
            colt[pl.ds(start, 128), :] = profile(own_col, (b * 128).astype(F32), 128)
            rowt[pl.ds(start, 128), :] = profile(own_row, (b * 128).astype(F32), 128)

        load_r.wait()
        load_c.wait()

        @pl.loop(0, 4)
        def _(b):
            start = pl.multiple_of(b * 128, 128)
            cols = pl.ds(start, 128)
            high, low = split(mc[:, cols])
            value = tn(high, colt[...]) + tn(low, colt[...])
            bth[cols, :] = value.astype(BF16)
            high, low = split(mr[:, cols])
            at[cols, :] = tn(high, rowt[...]) + tn(low, rowt[...])
            high, low = split(mc[cols, :])
            mch[cols, :] = high
            mcl[cols, :] = low

    def rows_of(who):
        return pl.ds(pl.multiple_of(who * 64, 64), 64)

    own = rows_of(v)

    def share_copy(s, o):
        src = sg.at[s, own, :]
        where = mate if o == 0 else (((x + o) % 4) * 2 + core, me)
        return remote(src, src, asem_s.at[s, o], asem_r.at[s, o], where)

    def share_start(s):
        sg[s, own, :] = sblk[:, s * 256 : s * 256 + 256].astype(BF16)
        for o in (2, 1, 3, 0):
            share_copy(s, o).start()

    def came(s, o, base, half):
        rows = rows_of(((x - o + 4) % 4) * 2 + half)
        block = sg.at[s, rows, :]
        where = (((x + o) % 4) * 2 + core, me) if base == 0 else mate
        return remote(block, block, asem_s.at[s, base + o], asem_r.at[s, base + o], where)

    def share_pass(s):
        for o in (1, 3, 2):
            came(s, o, 0, core).wait()
            block = sg.at[s, rows_of(((x - o + 4) % 4) * 2 + core), :]
            remote(block, block, asem_s.at[s, 4 + o], asem_r.at[s, 4 + o], mate).start()

    def share_end(s):
        came(s, 0, 0, other).wait()
        for o in (1, 3, 2):
            came(s, o, 4, other).wait()

    def own_flux(s):
        cols = slice(s * 256, s * 256 + 256)
        high, low = split(sblk[:, cols])
        value = nn(jnp.concatenate([high, low], axis=0), bth[cols, :])
        return value[0:64] + value[64:128]

    warp(0, 6, 2)
    warp(6, TD, 1)
    pl.semaphore_wait(barrier, peers)
    combine(other, 0)
    core_start(0)
    gather_start(metag, 0)
    combine(other, 1)
    core_start(1)
    load_r.start()
    load_c.start()
    combine(core, 0)
    core_add(0)
    combine(core, 1)
    core_add(1)
    gather_wait(metag, 0)
    measure(0, 2)
    advance(0, 0)
    measure(2, 4)
    advance(1, 0)
    measure(4, 6)
    advance(0, 1)
    gather_start(infog, 3)
    measure(6, 7)
    advance(1, 1)
    measure(7, 8)
    fluxg[me] = fluxo[...].astype(BF16)
    tables()
    advance(0, 2)
    gather_wait(infog, 3)
    info = infog[...].reshape(128, 128)
    mine = (info == me.astype(F32)) & (lax.broadcasted_iota(jnp.int32, (128, 128), 1) < 64)
    weights = jnp.where(mine, pltpu.roll(info, 64, 1), 0.0)
    weight_sum = jnp.sum(jnp.sum(weights, axis=0, keepdims=True), axis=1, keepdims=True) * (1.0 / 64.0)
    pg[v, 4:5, :] = jnp.broadcast_to(weight_sum, (1, 128))
    pg[v, 5:8, :] = jnp.zeros((3, 128), F32)
    advance(1, 2)

    gather_start(fluxg, 1)
    finish(0)
    share_start(0)
    value[...] = own_flux(0)
    finish(1)
    share_start(1)
    partial = jnp.sum((value[...] + own_flux(1)) * at[own, :], axis=0, keepdims=True)
    for c in range(4):
        pg[v, c : c + 1, :] = partial[:, c * 128 : (c + 1) * 128]

    @pl.loop(1, NV)
    def _(o):
        remote(pg.at[v], pg.at[v], vsem_s.at[o], vsem_r.at[o], ((v + o) % NV, me)).start()

    share_pass(0)
    gather_wait(fluxg, 1)
    tile = lax.broadcasted_iota(jnp.int32, (128, 128), 0)
    lane = lax.broadcasted_iota(jnp.int32, (128, 128), 1)
    hits = (infog[...].reshape(128, 128) == (lane % 16).astype(F32)) & (tile % 4 == lane // 16)
    hits = jnp.where(hits, 1.0, 0.0).astype(BF16)
    sums[...] = tn(hits, fluxg[...].reshape(128, S))
    counts[...] = tn(hits, jnp.ones((128, 128), BF16))

    @pl.loop(1, NV)
    def _(o):
        theirs = (v - o + NV) % NV
        remote(pg.at[theirs], pg.at[theirs], vsem_s.at[o], vsem_r.at[o], ((v + o) % NV, me)).wait()

    total = jnp.sum(pg[...], axis=0)
    inverse = 1.0 / total[4:5, :]
    refg[me] = total * inverse
    gather_start(refg, 2)

    share_pass(1)
    mrow_high, mrow_low = split(mr[own, :])
    both = jnp.concatenate([mrow_high, mrow_low], axis=0)
    matched = jnp.zeros((64, S), F32)
    for s in range(2):
        share_end(s)
        cols = slice(s * 256, s * 256 + 256)
        half = nn(both, sg[s])
        high, low = split(half[0:64] + half[64:128])
        pair = nt(jnp.concatenate([high, low], axis=0), mch[:, cols])
        matched = matched + pair[0:64] + pair[64:128] + nt(high, mcl[:, cols])
    for c in range(4):
        coadd_ref[:, c * 128 : (c + 1) * 128] = matched[:, c * 128 : (c + 1) * 128] * inverse

    gather_wait(refg, 2)
    refs = jnp.concatenate([refg[:, c, :] for c in range(4)], axis=1)
    squares = jnp.sum(refs * refs, axis=1, keepdims=True)
    fits = []
    for u in range(4):
        rows = slice(u * 16, u * 16 + 16)
        top = jnp.sum(jnp.sum(sums[rows, :] * refs, axis=0, keepdims=True), axis=1, keepdims=True)
        low = jnp.sum(counts[rows, 0:1] * squares, axis=0, keepdims=True)
        fits.append(top / low)
    for u in range(4):
        zp_ref[u : u + 1, :] = jnp.broadcast_to(fits[u], (1, 128))
    for t in range(TD):
        q = patch_sm[t]
        template = jnp.concatenate([refg[q, c : c + 1, :] for c in range(4)], axis=1)
        resid_ref[t : t + 1, :] = fluxo[t : t + 1, :] - fits[t % 4] * template


def fused(tile_patch, tile_weight, images, warp_rows, warp_cols, match_rows, match_cols, src_row, src_col):
    dma = pltpu.SemaphoreType.DMA
    any_ = pl.BlockSpec(memory_space=pl.ANY)
    smem = pl.BlockSpec(memory_space=pltpu.SMEM)
    vmem = pl.BlockSpec(memory_space=pltpu.VMEM)
    return pl.pallas_call(
        kernel,
        out_shape=(
            jax.ShapeDtypeStruct((64, S), F32),
            jax.ShapeDtypeStruct((4, 128), F32),
            jax.ShapeDtypeStruct((TD, S), F32),
        ),
        in_specs=[smem, vmem, any_, any_, any_, any_, any_, vmem, vmem],
        out_specs=(vmem, vmem, vmem),
        scratch_shapes=[
            pltpu.VMEM((TD, S, S), BF16),
            pltpu.VMEM((TD, S, S), BF16),
            pltpu.VMEM((TD, S, S), BF16),
            pltpu.VMEM((2, S, S), BF16),
            pltpu.VMEM((TD, S, S), BF16),
            pltpu.VMEM((S, S), F32),
            pltpu.VMEM((S, S), F32),
            pltpu.VMEM((2, 64 * 16, 16, 128), BF16),
            pltpu.VMEM((64 * 16, 16, 128), BF16),
            pltpu.VMEM((32 * 16, 16, 128), BF16),
            pltpu.VMEM((16 * 16, 16, 128), BF16),
            pltpu.VMEM((8 * 16, 16, 128), BF16),
            pltpu.VMEM((8 * 16, 16, 128), BF16),
            pltpu.VMEM((128, S), F32),
            pltpu.VMEM((128, 128), F32),
            pltpu.VMEM((64, S), F32),
            pltpu.VMEM((NP, 8, 128), F32),
            pltpu.VMEM((NP, TD, 128), F32),
            pltpu.VMEM((NP, TD, S), BF16),
            pltpu.VMEM((TD, S), F32),
            pltpu.VMEM((NV, 8, 128), F32),
            pltpu.VMEM((NP, 8, 128), F32),
            pltpu.VMEM((2, S, 256), BF16),
            pltpu.VMEM((S, S), BF16),
            pltpu.VMEM((S, S), BF16),
            pltpu.VMEM((S, S), BF16),
            pltpu.VMEM((S, S), F32),
            pltpu.VMEM((S, S), BF16),
            pltpu.VMEM((S, S), BF16),
            pltpu.VMEM((64, S), F32),
            pltpu.SMEM((2 * NP,), jnp.int32),
            pltpu.SMEM((2 * NP,), F32),
            pltpu.SMEM((TD,), F32),
            dma((3, TD)), dma((3,)), dma((2, 6)), dma((2, 6)), dma((3, 12)), dma((3, 12)), dma((12, 8)), dma((12, 8)),
            dma((4, NP)), dma((4, NP)), dma((NV,)), dma((NV,)), dma((2, 8)), dma((2, 8)),
        ],
        compiler_params=pltpu.CompilerParams(
            collective_id=0, has_side_effects=True, vmem_limit_bytes=60 * 1024 * 1024
        ),
        name="coadd",
    )(tile_patch, tile_weight, images, warp_rows, warp_cols, match_rows, match_cols, src_row, src_col)


def store(coadd_in, zp_in, resid_in, coadd_ref, zp_ref, resid_ref):
    coadd_ref[0] = coadd_in[...]
    resid_ref[...] = resid_in[...]
    for u in range(4):
        zp_ref[u] = jnp.max(zp_in[u : u + 1, :])


def shards(
    images, warp_rows, warp_cols, tile_weight, tile_patch, match_rows, match_cols, src_row, src_col
):
    coadd, zero_point, resid = fused(
        tile_patch, tile_weight[None], images, warp_rows, warp_cols, match_rows[0], match_cols[0], src_row, src_col
    )
    vmem = pl.BlockSpec(memory_space=pltpu.VMEM)
    return pl.pallas_call(
        store,
        out_shape=(
            jax.ShapeDtypeStruct((1, 64, S), F32),
            jax.ShapeDtypeStruct((4,), F32),
            jax.ShapeDtypeStruct((TD, S), F32),
        ),
        in_specs=[vmem, vmem, vmem],
        out_specs=(vmem, pl.BlockSpec(memory_space=pltpu.SMEM), vmem),
        name="store",
    )(coadd, zero_point, resid)


def solution(mesh):
    in_specs = (
        P(("visit", "patch"), None, None),
        P(("visit", "patch"), None, None),
        P(("visit", "patch"), None, None),
        P(("visit", "patch")),
        P(("visit", "patch")),
        P("patch", None, None),
        P("patch", None, None),
        P("patch", None),
        P("patch", None),
    )
    out_specs = (P("patch", "visit", None), P("visit"), P(("visit", "patch"), None))
    return jax.shard_map(shards, mesh=mesh, in_specs=in_specs, out_specs=out_specs, check_vma=False)
```

```python
import jax
import jax.numpy as jnp
from jax import lax
from jax.experimental import pallas as pl
from jax.experimental.pallas import tpu as pltpu
from jax.sharding import PartitionSpec as P

F32 = jnp.float32
BF16 = jnp.bfloat16
S = 512
NP = 16
NV = 8
TD = 8
MESH = pl.DeviceIdType.MESH

ORDER = ("x0", "y0", "z0", "x1", "y1", "z1")
UNITS = (((0, 1), (2, 3), (4, 5), (6, 7), (8,), (9,)), ((10,), (11,), (12,), (13,), (14,), (15,)))


def gray(c):
    return c // 2, (c // 2 + c % 2) % 2


def nt(a, b):
    return lax.dot_general(a, b, (((1,), (1,)), ((), ())), preferred_element_type=F32)


def tn(a, b):
    return lax.dot_general(a, b, (((0,), (0,)), ((), ())), preferred_element_type=F32)


def nn(a, b):
    return jnp.dot(a, b, preferred_element_type=F32)


def split(a):
    high = a.astype(BF16)
    return high, (a - high.astype(F32)).astype(BF16)


def profile(center, first, count):
    pixel = lax.broadcasted_iota(jnp.int32, (count, S), 0).astype(F32) + first
    distance = pixel - center
    return jnp.exp(distance * distance * (-1.0 / 12.5)).astype(BF16)


def kernel(
    patch_sm, weight_ref, img_hbm, wr_hbm, wc_hbm, mr_hbm, mc_hbm, srow_ref, scol_ref,
    coadd_ref, zp_ref, resid_ref,
    img, wr, wc, halfs, warped, mr, mc, acc, rc, r0, r1, r2, fin, sums, counts, value,
    metag, infog, fluxg, fluxo, pg, refg, sg, colt, rowt, bth, at, mch, mcl, sblk,
    tab_i, tab_w, weight_sm, tsem, lsem, csem_s, csem_r, rsem_s, rsem_r, fsem_s, fsem_r, gsem_s, gsem_r, vsem_s, vsem_r, asem_s, asem_r,
):
    v = lax.axis_index("visit")
    me = lax.axis_index("patch")
    x, core = v // 2, v % 2
    y, z = me // 4, me % 4
    side = {}
    for name, c in (("x", x), ("y", y), ("z", z)):
        side[name + "1"], side[name + "0"] = gray(c)
    flip0 = lambda c: c + 1 - 2 * (c % 2)
    partner = {
        "x0": (flip0(x) * 2 + core, me), "x1": ((3 - x) * 2 + core, me),
        "y0": (v, flip0(y) * 4 + z), "y1": (v, (3 - y) * 4 + z),
        "z0": (v, y * 4 + flip0(z)), "z1": (v, y * 4 + 3 - z),
    }
    other = 1 - core
    mate = (x * 2 + other, me)

    def remote(src, dst, ss, rs, where):
        return pltpu.make_async_remote_copy(
            src_ref=src, dst_ref=dst, send_sem=ss, recv_sem=rs,
            device_id={"visit": where[0], "patch": where[1]}, device_id_type=MESH,
        )

    barrier = pltpu.get_barrier_semaphore()

    @pl.loop(1, NP)
    def _(o):
        pl.semaphore_signal(barrier, inc=1, device_id={"visit": v, "patch": (me + o) % NP}, device_id_type=MESH)

    @pl.loop(1, NV)
    def _(o):
        pl.semaphore_signal(barrier, inc=1, device_id={"visit": (v + o) % NV, "patch": me}, device_id_type=MESH)

    flips = {"x": (flip0(x), 3 - x), "y": (flip0(y), 3 - y), "z": (flip0(z), 3 - z)}
    met = set()
    for k in range(6):
        last = tuple(sorted(ORDER[(k + 3 + i) % 6] for i in range(3)))
        met |= {last, last[:2], (last[0], last[2])}
    for dims in sorted(met):
        where = {"x": x, "y": y, "z": z}
        for d in dims:
            where[d[0]] = flips[d[0]][int(d[1])]
        there = {"visit": where["x"] * 2 + core, "patch": where["y"] * 4 + where["z"]}
        pl.semaphore_signal(barrier, inc=1, device_id=there, device_id_type=MESH)
    peers = NP - 1 + NV - 1 + len(met)

    def tile_load(i, t):
        hbm, buf = ((wc_hbm, wc), (img_hbm, img), (wr_hbm, wr))[i]
        return pltpu.make_async_copy(hbm.at[t], buf.at[t], tsem.at[i, t])

    @pl.loop(0, TD)
    def _(t):
        for i in range(3):
            tile_load(i, t).start()

    load_r = pltpu.make_async_copy(mr_hbm, mr, lsem.at[1])
    load_c = pltpu.make_async_copy(mc_hbm, mc, lsem.at[2])

    lane8 = lax.broadcasted_iota(jnp.int32, (1, TD), 1)
    for t in range(TD):
        weight_sm[t] = jnp.sum(jnp.where(lane8 == t, weight_ref[...].astype(F32), 0.0))

    @pl.loop(0, NP)
    def _(p):
        ia = jnp.int32(0)
        ib = jnp.int32(0)
        wa = jnp.float32(0)
        wb = jnp.float32(0)
        seen = jnp.int32(0)
        for t in range(TD):
            hit = (patch_sm[t] == p).astype(jnp.int32)
            first = hit * (1 - jnp.minimum(seen, 1))
            second = hit * (seen == 1).astype(jnp.int32)
            ia = ia + first * t
            ib = ib + second * t
            wa = wa + first.astype(F32) * weight_sm[t]
            wb = wb + second.astype(F32) * weight_sm[t]
            seen = seen + hit
        tab_i[p] = ia
        tab_i[NP + p] = ib
        tab_w[p] = wa
        tab_w[NP + p] = wb

    low_lanes = lax.broadcasted_iota(jnp.int32, (1, 128), 1) < 64
    for t in range(TD):
        infog[me, t : t + 1, :] = jnp.where(low_lanes, patch_sm[t].astype(F32), weight_sm[t])
    for c in range(4):
        metag[me, c : 1 + c, :] = srow_ref[:, c * 128 : (c + 1) * 128].astype(F32)
        metag[me, 4 + c : 5 + c, :] = scol_ref[:, c * 128 : (c + 1) * 128].astype(F32)

    def gather_copy(buf, kind, o):
        return remote(buf.at[me], buf.at[me], gsem_s.at[kind, o], gsem_r.at[kind, o], (v, (me + o) % NP))

    def gather_start(buf, kind):
        @pl.loop(1, NP)
        def _(o):
            gather_copy(buf, kind, o).start()

    def gather_wait(buf, kind):
        @pl.loop(1, NP)
        def _(o):
            theirs = (me - o + NP) % NP
            remote(buf.at[theirs], buf.at[theirs], gsem_s.at[kind, o], gsem_r.at[kind, o], (v, (me + o) % NP)).wait()

    def warp(first, last, step):
        @pl.loop(first // step, last // step)
        def _(tt):
            for i in range(step):
                t = tt * step + i
                for n in range(2):
                    tile_load(n, t).wait()
                halfs[i] = nt(img[t], wc[t]).astype(BF16)
            for i in range(step):
                t = tt * step + i
                tile_load(2, t).wait()
                warped[t] = nn(wr[t], halfs[i]).astype(BF16)

    def combine(h, s):
        @pl.loop(0, NP)
        def _(p):
            ia, ib = tab_i[p], tab_i[NP + p]
            wa = jnp.full((16, 128), tab_w[p], F32).astype(BF16)
            wb = jnp.full((16, 128), tab_w[NP + p], F32).astype(BF16)
            bits = {}
            bits["y1"], bits["y0"] = gray(p // 4)
            bits["z1"], bits["z0"] = gray(p % 4)
            starts = []
            for k in range(6):
                place = 0
                for j in range(6):
                    d = ORDER[(k + j) % 6]
                    if d[0] != "x":
                        place = place + bits[d] * (32 >> j)
                starts.append(place * len(UNITS[s][k]) + UNITS[s][k][0] * 64)
            for xr in range(4):
                bits["x1"], bits["x0"] = gray(xr)
                for k in range(6):
                    shift = 0
                    for j in range(6):
                        d = ORDER[(k + j) % 6]
                        if d[0] == "x":
                            shift += bits[d] * (32 >> j)
                    for i, unit in enumerate(UNITS[s][k]):
                        rows = pl.ds(pl.multiple_of((xr * 2 + h) * 64 + unit % 4 * 16, 16), 16)
                        lanes = slice(unit // 4 * 128, unit // 4 * 128 + 128)
                        acc[h, starts[k] + shift * len(UNITS[s][k]) + i] = (
                            warped[ia, rows, lanes] * wa + warped[ib, rows, lanes] * wb
                        )

    def part(s, k, total, start, count):
        n = len(UNITS[s][k])
        return pl.ds(UNITS[s][k][0] * total + start * n, count * n)

    def core_copy(s, k):
        span = part(s, k, 64, 0, 64)
        return remote(acc.at[other, span], rc.at[span], csem_s.at[s, k], csem_r.at[s, k], mate)

    def core_start(s):
        for k in range(6):
            core_copy(s, k).start()

    def source_lines(q, first):
        return jnp.concatenate([metag[q, first + c : first + c + 1, :] for c in range(4)], axis=1)

    def measure(first, last):
        @pl.loop(first, last)
        def _(t):
            q = patch_sm[t]
            row_of = source_lines(q, 0)
            col_of = source_lines(q, 4)

            @pl.loop(0, 4)
            def _(b):
                start = pl.multiple_of(b * 128, 128)
                colt[pl.ds(start, 128), :] = profile(col_of, (b * 128).astype(F32), 128)

            def part(b, total):
                start = pl.multiple_of(b * 128, 128)
                by_col = nn(warped[t, pl.ds(start, 128), :], colt[...])
                rows = profile(row_of, (b * 128).astype(F32), 128).astype(F32)
                return total + jnp.sum((by_col * rows).reshape(16, 8, S), axis=0)

            total = lax.fori_loop(0, 4, part, jnp.zeros((8, S), F32))
            fluxo[pl.ds(t, 1), :] = jnp.sum(total, axis=0, keepdims=True)

    bufs = (r0, r1, r2)

    def base_of(k, j):
        base = 0
        for i in range(j):
            base = base + side[ORDER[(k + i) % 6]] * (32 >> i)
        return base

    def round_copy(s, k, j):
        d = ORDER[(k + j) % 6]
        half = 32 >> j
        start = base_of(k, j) + (1 - side[d]) * half
        src = acc.at[core, part(s, k, 64, start, half)]
        dst = bufs[j].at[part(s, k, half, 0, half)]
        return remote(src, dst, rsem_s.at[j, s * 6 + k], rsem_r.at[j, s * 6 + k], partner[d])

    def round_add(s, k, j):
        half = 32 >> j
        step = min(half, 16)

        @pl.loop(0, half // step)
        def _(i):
            at_ = part(s, k, 64, base_of(k, j + 1) + i * step, step)
            acc[core, at_] = acc[core, at_] + bufs[j][part(s, k, half, i * step, step)]

    def last_copy(s, k, e):
        place = base_of(k, 3)
        where = {"x": x, "y": y, "z": z}
        for i in range(3):
            d = ORDER[(k + 3 + i) % 6]
            bit = side[d]
            if e >> (2 - i) & 1:
                bit = 1 - bit
                c = where[d[0]]
                where[d[0]] = flip0(c) if d[1] == "0" else 3 - c
            place = place + bit * (4 >> i)
        there = (where["x"] * 2 + core, where["y"] * 4 + where["z"])
        return remote(
            acc.at[core, part(s, k, 64, place, 1)], fin.at[part(s, k, 8, e, 1)],
            fsem_s.at[s * 6 + k, e], fsem_r.at[s * 6 + k, e], there,
        )

    def core_add(s):
        for k in range(6):
            core_copy(s, k).wait()

            @pl.loop(0, 4)
            def _(i):
                at_ = part(s, k, 64, i * 16, 16)
                acc[core, at_] = acc[core, at_] + rc[at_]

            round_copy(s, k, 0).start()

    def advance(s, j):
        for k in range(6):
            round_copy(s, k, j).wait()
            round_add(s, k, j)
            if j < 2:
                round_copy(s, k, j + 1).start()
            else:
                for e in (7, 6, 5, 3, 4, 2, 1):
                    last_copy(s, k, e).start()

    def finish(s):
        for k in range(6):
            n = len(UNITS[s][k])
            place = base_of(k, 6)
            for e in (1, 2, 4, 3, 5, 6, 7):
                last_copy(s, k, e).wait()
            for i, unit in enumerate(UNITS[s][k]):
                value = acc[core, UNITS[s][k][0] * 64 + place * n + i].astype(F32)
                for e in range(1, 8):
                    value = value + fin[UNITS[s][k][0] * 8 + e * n + i].astype(F32)
                lanes = slice(unit // 4 * 128, unit // 4 * 128 + 128)
                sblk[unit % 4 * 16 : unit % 4 * 16 + 16, lanes] = value

    def tables():
        own_row = source_lines(me, 0)
        own_col = source_lines(me, 4)

        @pl.loop(0, 4)
        def _(b):
            start = pl.multiple_of(b * 128, 128)
            colt[pl.ds(start, 128), :] = profile(own_col, (b * 128).astype(F32), 128)
            rowt[pl.ds(start, 128), :] = profile(own_row, (b * 128).astype(F32), 128)

        load_r.wait()
        load_c.wait()

        @pl.loop(0, 4)
        def _(b):
            start = pl.multiple_of(b * 128, 128)
            cols = pl.ds(start, 128)
            high, low = split(mc[:, cols])
            value = tn(high, colt[...]) + tn(low, colt[...])
            bth[cols, :] = value.astype(BF16)
            high, low = split(mr[:, cols])
            at[cols, :] = tn(high, rowt[...]) + tn(low, rowt[...])
            high, low = split(mc[cols, :])
            mch[cols, :] = high
            mcl[cols, :] = low

    def rows_of(who):
        return pl.ds(pl.multiple_of(who * 64, 64), 64)

    own = rows_of(v)

    def share_copy(s, o):
        src = sg.at[s, own, :]
        where = mate if o == 0 else (((x + o) % 4) * 2 + core, me)
        return remote(src, src, asem_s.at[s, o], asem_r.at[s, o], where)

    def share_start(s):
        sg[s, own, :] = sblk[:, s * 256 : s * 256 + 256].astype(BF16)
        for o in (2, 1, 3, 0):
            share_copy(s, o).start()

    def came(s, o, base, half):
        rows = rows_of(((x - o + 4) % 4) * 2 + half)
        block = sg.at[s, rows, :]
        where = (((x + o) % 4) * 2 + core, me) if base == 0 else mate
        return remote(block, block, asem_s.at[s, base + o], asem_r.at[s, base + o], where)

    def share_pass(s):
        for o in (1, 3, 2):
            came(s, o, 0, core).wait()
            block = sg.at[s, rows_of(((x - o + 4) % 4) * 2 + core), :]
            remote(block, block, asem_s.at[s, 4 + o], asem_r.at[s, 4 + o], mate).start()

    def share_end(s):
        came(s, 0, 0, other).wait()
        for o in (1, 3, 2):
            came(s, o, 4, other).wait()

    def own_flux(s):
        cols = slice(s * 256, s * 256 + 256)
        high, low = split(sblk[:, cols])
        value = nn(jnp.concatenate([high, low], axis=0), bth[cols, :])
        return value[0:64] + value[64:128]

    warp(0, 6, 2)
    warp(6, TD, 1)
    pl.semaphore_wait(barrier, peers)
    combine(other, 0)
    core_start(0)
    gather_start(metag, 0)
    combine(other, 1)
    core_start(1)
    load_r.start()
    load_c.start()
    combine(core, 0)
    core_add(0)
    combine(core, 1)
    core_add(1)
    gather_wait(metag, 0)
    measure(0, 2)
    advance(0, 0)
    measure(2, 4)
    advance(1, 0)
    measure(4, 6)
    advance(0, 1)
    gather_start(infog, 3)
    measure(6, 7)
    advance(1, 1)
    measure(7, 8)
    fluxg[me] = fluxo[...].astype(BF16)
    tables()
    advance(0, 2)
    gather_wait(infog, 3)
    info = infog[...].reshape(128, 128)
    mine = (info == me.astype(F32)) & (lax.broadcasted_iota(jnp.int32, (128, 128), 1) < 64)
    weights = jnp.where(mine, pltpu.roll(info, 64, 1), 0.0)
    weight_sum = jnp.sum(jnp.sum(weights, axis=0, keepdims=True), axis=1, keepdims=True) * (1.0 / 64.0)
    pg[v, 4:5, :] = jnp.broadcast_to(weight_sum, (1, 128))
    pg[v, 5:8, :] = jnp.zeros((3, 128), F32)
    advance(1, 2)

    gather_start(fluxg, 1)
    finish(0)
    share_start(0)
    value[...] = own_flux(0)
    finish(1)
    share_start(1)
    partial = jnp.sum((value[...] + own_flux(1)) * at[own, :], axis=0, keepdims=True)
    for c in range(4):
        pg[v, c : c + 1, :] = partial[:, c * 128 : (c + 1) * 128]

    @pl.loop(1, NV)
    def _(o):
        remote(pg.at[v], pg.at[v], vsem_s.at[o], vsem_r.at[o], ((v + o) % NV, me)).start()

    share_pass(0)
    gather_wait(fluxg, 1)
    tile = lax.broadcasted_iota(jnp.int32, (128, 128), 0)
    lane = lax.broadcasted_iota(jnp.int32, (128, 128), 1)
    hits = (infog[...].reshape(128, 128) == (lane % 16).astype(F32)) & (tile % 4 == lane // 16)
    hits = jnp.where(hits, 1.0, 0.0).astype(BF16)
    sums[...] = tn(hits, fluxg[...].reshape(128, S))
    counts[...] = tn(hits, jnp.ones((128, 128), BF16))

    @pl.loop(1, NV)
    def _(o):
        theirs = (v - o + NV) % NV
        remote(pg.at[theirs], pg.at[theirs], vsem_s.at[o], vsem_r.at[o], ((v + o) % NV, me)).wait()

    total = jnp.sum(pg[...], axis=0)
    inverse = 1.0 / total[4:5, :]
    refg[me] = total * inverse
    gather_start(refg, 2)

    share_pass(1)
    mrow_high, mrow_low = split(mr[own, :])
    both = jnp.concatenate([mrow_high, mrow_low], axis=0)
    matched = jnp.zeros((64, S), F32)
    for s in range(2):
        share_end(s)
        cols = slice(s * 256, s * 256 + 256)
        half = nn(both, sg[s])
        high, low = split(half[0:64] + half[64:128])
        pair = nt(jnp.concatenate([high, low], axis=0), mch[:, cols])
        matched = matched + pair[0:64] + pair[64:128] + nt(high, mcl[:, cols])
    for c in range(4):
        coadd_ref[:, c * 128 : (c + 1) * 128] = matched[:, c * 128 : (c + 1) * 128] * inverse

    gather_wait(refg, 2)
    refs = jnp.concatenate([refg[:, c, :] for c in range(4)], axis=1)
    squares = jnp.sum(refs * refs, axis=1, keepdims=True)
    fits = []
    for u in range(4):
        rows = slice(u * 16, u * 16 + 16)
        top = jnp.sum(jnp.sum(sums[rows, :] * refs, axis=0, keepdims=True), axis=1, keepdims=True)
        low = jnp.sum(counts[rows, 0:1] * squares, axis=0, keepdims=True)
        fits.append(top / low)
    for u in range(4):
        zp_ref[u : u + 1, :] = jnp.broadcast_to(fits[u], (1, 128))
    for t in range(TD):
        q = patch_sm[t]
        template = jnp.concatenate([refg[q, c : c + 1, :] for c in range(4)], axis=1)
        resid_ref[t : t + 1, :] = fluxo[t : t + 1, :] - fits[t % 4] * template


def fused(tile_patch, tile_weight, images, warp_rows, warp_cols, match_rows, match_cols, src_row, src_col):
    dma = pltpu.SemaphoreType.DMA
    any_ = pl.BlockSpec(memory_space=pl.ANY)
    smem = pl.BlockSpec(memory_space=pltpu.SMEM)
    vmem = pl.BlockSpec(memory_space=pltpu.VMEM)
    return pl.pallas_call(
        kernel,
        out_shape=(
            jax.ShapeDtypeStruct((64, S), F32),
            jax.ShapeDtypeStruct((4, 128), F32),
            jax.ShapeDtypeStruct((TD, S), F32),
        ),
        in_specs=[smem, vmem, any_, any_, any_, any_, any_, vmem, vmem],
        out_specs=(vmem, vmem, vmem),
        scratch_shapes=[
            pltpu.VMEM((TD, S, S), BF16),
            pltpu.VMEM((TD, S, S), BF16),
            pltpu.VMEM((TD, S, S), BF16),
            pltpu.VMEM((2, S, S), BF16),
            pltpu.VMEM((TD, S, S), BF16),
            pltpu.VMEM((S, S), F32),
            pltpu.VMEM((S, S), F32),
            pltpu.VMEM((2, 64 * 16, 16, 128), BF16),
            pltpu.VMEM((64 * 16, 16, 128), BF16),
            pltpu.VMEM((32 * 16, 16, 128), BF16),
            pltpu.VMEM((16 * 16, 16, 128), BF16),
            pltpu.VMEM((8 * 16, 16, 128), BF16),
            pltpu.VMEM((8 * 16, 16, 128), BF16),
            pltpu.VMEM((128, S), F32),
            pltpu.VMEM((128, 128), F32),
            pltpu.VMEM((64, S), F32),
            pltpu.VMEM((NP, 8, 128), F32),
            pltpu.VMEM((NP, TD, 128), F32),
            pltpu.VMEM((NP, TD, S), BF16),
            pltpu.VMEM((TD, S), F32),
            pltpu.VMEM((NV, 8, 128), F32),
            pltpu.VMEM((NP, 8, 128), F32),
            pltpu.VMEM((2, S, 256), BF16),
            pltpu.VMEM((S, S), BF16),
            pltpu.VMEM((S, S), BF16),
            pltpu.VMEM((S, S), BF16),
            pltpu.VMEM((S, S), F32),
            pltpu.VMEM((S, S), BF16),
            pltpu.VMEM((S, S), BF16),
            pltpu.VMEM((64, S), F32),
            pltpu.SMEM((2 * NP,), jnp.int32),
            pltpu.SMEM((2 * NP,), F32),
            pltpu.SMEM((TD,), F32),
            dma((3, TD)), dma((3,)), dma((2, 6)), dma((2, 6)), dma((3, 12)), dma((3, 12)), dma((12, 8)), dma((12, 8)),
            dma((4, NP)), dma((4, NP)), dma((NV,)), dma((NV,)), dma((2, 8)), dma((2, 8)),
        ],
        compiler_params=pltpu.CompilerParams(
            collective_id=0, has_side_effects=True, vmem_limit_bytes=60 * 1024 * 1024
        ),
        name="coadd",
    )(tile_patch, tile_weight, images, warp_rows, warp_cols, match_rows, match_cols, src_row, src_col)


def store(coadd_in, zp_in, resid_in, coadd_ref, zp_ref, resid_ref):
    coadd_ref[0] = coadd_in[...]
    resid_ref[...] = resid_in[...]
    for u in range(4):
        zp_ref[u] = jnp.max(zp_in[u : u + 1, :])


def shards(
    images, warp_rows, warp_cols, tile_weight, tile_patch, match_rows, match_cols, src_row, src_col
):
    coadd, zero_point, resid = fused(
        tile_patch, tile_weight[None], images, warp_rows, warp_cols, match_rows[0], match_cols[0], src_row, src_col
    )
    vmem = pl.BlockSpec(memory_space=pltpu.VMEM)
    return pl.pallas_call(
        store,
        out_shape=(
            jax.ShapeDtypeStruct((1, 64, S), F32),
            jax.ShapeDtypeStruct((4,), F32),
            jax.ShapeDtypeStruct((TD, S), F32),
        ),
        in_specs=[vmem, vmem, vmem],
        out_specs=(vmem, pl.BlockSpec(memory_space=pltpu.SMEM), vmem),
        name="store",
    )(coadd, zero_point, resid)


def solution(mesh):
    in_specs = (
        P(("visit", "patch"), None, None),
        P(("visit", "patch"), None, None),
        P(("visit", "patch"), None, None),
        P(("visit", "patch")),
        P(("visit", "patch")),
        P("patch", None, None),
        P("patch", None, None),
        P("patch", None),
        P("patch", None),
    )
    out_specs = (P("patch", "visit", None), P("visit"), P(("visit", "patch"), None))
    return jax.shard_map(shards, mesh=mesh, in_specs=in_specs, out_specs=out_specs, check_vma=False)
```

```python
import jax
import jax.numpy as jnp
from jax import lax
from jax.experimental import pallas as pl
from jax.experimental.pallas import tpu as pltpu
from jax.sharding import PartitionSpec as P

F32 = jnp.float32
BF16 = jnp.bfloat16
S = 512
NP = 16
NV = 8
TD = 8
MESH = pl.DeviceIdType.MESH

ORDER = ("x0", "y0", "z0", "x1", "y1", "z1")
UNITS = (((0, 1), (2, 3), (4,), (5,), (6,), (7,)), ((8,), (9,), (10, 11), (12, 13), (14,), (15,)))


def gray(c):
    return c // 2, (c // 2 + c % 2) % 2


def nt(a, b):
    return lax.dot_general(a, b, (((1,), (1,)), ((), ())), preferred_element_type=F32)


def tn(a, b):
    return lax.dot_general(a, b, (((0,), (0,)), ((), ())), preferred_element_type=F32)


def nn(a, b):
    return jnp.dot(a, b, preferred_element_type=F32)


def split(a):
    high = a.astype(BF16)
    return high, (a - high.astype(F32)).astype(BF16)


def profile(center, first, count):
    pixel = lax.broadcasted_iota(jnp.int32, (count, S), 0).astype(F32) + first
    distance = pixel - center
    return jnp.exp(distance * distance * (-1.0 / 12.5)).astype(BF16)


def kernel(
    patch_sm, weight_ref, img_hbm, wr_hbm, wc_hbm, mr_hbm, mc_hbm, srow_ref, scol_ref,
    coadd_ref, zp_ref, resid_ref,
    img, wr, wc, halfs, warped, mr, mc, acc, rc, r0, r1, r2, fin, sums, counts, value,
    metag, infog, fluxg, fluxo, pg, refg, sg, colt, rowt, bth, at, mch, mcl, sblk,
    tab_i, tab_w, weight_sm, tsem, lsem, csem_s, csem_r, rsem_s, rsem_r, fsem_s, fsem_r, gsem_s, gsem_r, vsem_s, vsem_r, asem_s, asem_r,
):
    v = lax.axis_index("visit")
    me = lax.axis_index("patch")
    x, core = v // 2, v % 2
    y, z = me // 4, me % 4
    side = {}
    for name, c in (("x", x), ("y", y), ("z", z)):
        side[name + "1"], side[name + "0"] = gray(c)
    flip0 = lambda c: c + 1 - 2 * (c % 2)
    partner = {
        "x0": (flip0(x) * 2 + core, me), "x1": ((3 - x) * 2 + core, me),
        "y0": (v, flip0(y) * 4 + z), "y1": (v, (3 - y) * 4 + z),
        "z0": (v, y * 4 + flip0(z)), "z1": (v, y * 4 + 3 - z),
    }
    other = 1 - core
    mate = (x * 2 + other, me)

    def remote(src, dst, ss, rs, where):
        return pltpu.make_async_remote_copy(
            src_ref=src, dst_ref=dst, send_sem=ss, recv_sem=rs,
            device_id={"visit": where[0], "patch": where[1]}, device_id_type=MESH,
        )

    barrier = pltpu.get_barrier_semaphore()

    @pl.loop(1, NP)
    def _(o):
        pl.semaphore_signal(barrier, inc=1, device_id={"visit": v, "patch": (me + o) % NP}, device_id_type=MESH)

    @pl.loop(1, NV)
    def _(o):
        pl.semaphore_signal(barrier, inc=1, device_id={"visit": (v + o) % NV, "patch": me}, device_id_type=MESH)

    bases = {}
    for k in range(6):
        bases[k, 0] = 0
        for j in range(6):
            bases[k, j + 1] = bases[k, j] + side[ORDER[(k + j) % 6]] * (32 >> j)
    lasts = {}
    for k in range(6):
        for e in range(1, 8):
            place = bases[k, 3]
            where = {"x": x, "y": y, "z": z}
            for i in range(3):
                d = ORDER[(k + 3 + i) % 6]
                bit = side[d]
                if e >> (2 - i) & 1:
                    bit = 1 - bit
                    c = where[d[0]]
                    where[d[0]] = flip0(c) if d[1] == "0" else 3 - c
                place = place + bit * (4 >> i)
            lasts[k, e] = (place, (where["x"] * 2 + core, where["y"] * 4 + where["z"]))

    flips = {"x": (flip0(x), 3 - x), "y": (flip0(y), 3 - y), "z": (flip0(z), 3 - z)}
    met = set()
    for k in range(6):
        last = tuple(sorted(ORDER[(k + 3 + i) % 6] for i in range(3)))
        met |= {last, last[:2], (last[0], last[2])}
    for dims in sorted(met):
        where = {"x": x, "y": y, "z": z}
        for d in dims:
            where[d[0]] = flips[d[0]][int(d[1])]
        there = {"visit": where["x"] * 2 + core, "patch": where["y"] * 4 + where["z"]}
        pl.semaphore_signal(barrier, inc=1, device_id=there, device_id_type=MESH)
    peers = NP - 1 + NV - 1 + len(met)

    def tile_load(i, t):
        hbm, buf = ((wc_hbm, wc), (img_hbm, img), (wr_hbm, wr))[i]
        return pltpu.make_async_copy(hbm.at[t], buf.at[t], tsem.at[i, t])

    @pl.loop(0, TD)
    def _(t):
        for i in range(3):
            tile_load(i, t).start()

    load_r = pltpu.make_async_copy(mr_hbm, mr, lsem.at[1])
    load_c = pltpu.make_async_copy(mc_hbm, mc, lsem.at[2])

    lane8 = lax.broadcasted_iota(jnp.int32, (1, TD), 1)
    for t in range(TD):
        weight_sm[t] = jnp.sum(jnp.where(lane8 == t, weight_ref[...].astype(F32), 0.0))

    @pl.loop(0, NP)
    def _(p):
        ia = jnp.int32(0)
        ib = jnp.int32(0)
        wa = jnp.float32(0)
        wb = jnp.float32(0)
        seen = jnp.int32(0)
        for t in range(TD):
            hit = (patch_sm[t] == p).astype(jnp.int32)
            first = hit * (1 - jnp.minimum(seen, 1))
            second = hit * (seen == 1).astype(jnp.int32)
            ia = ia + first * t
            ib = ib + second * t
            wa = wa + first.astype(F32) * weight_sm[t]
            wb = wb + second.astype(F32) * weight_sm[t]
            seen = seen + hit
        tab_i[p] = ia
        tab_i[NP + p] = ib
        tab_w[p] = wa
        tab_w[NP + p] = wb

    low_lanes = lax.broadcasted_iota(jnp.int32, (1, 128), 1) < 64
    for t in range(TD):
        infog[me, t : t + 1, :] = jnp.where(low_lanes, patch_sm[t].astype(F32), weight_sm[t])
    for c in range(4):
        metag[me, c : 1 + c, :] = srow_ref[:, c * 128 : (c + 1) * 128].astype(F32)
        metag[me, 4 + c : 5 + c, :] = scol_ref[:, c * 128 : (c + 1) * 128].astype(F32)

    def gather_copy(buf, kind, o):
        return remote(buf.at[me], buf.at[me], gsem_s.at[kind, o], gsem_r.at[kind, o], (v, (me + o) % NP))

    def gather_start(buf, kind):
        @pl.loop(1, NP)
        def _(o):
            gather_copy(buf, kind, o).start()

    def gather_wait(buf, kind):
        @pl.loop(1, NP)
        def _(o):
            theirs = (me - o + NP) % NP
            remote(buf.at[theirs], buf.at[theirs], gsem_s.at[kind, o], gsem_r.at[kind, o], (v, (me + o) % NP)).wait()

    def warp(first, last, step):
        @pl.loop(first // step, last // step)
        def _(tt):
            for i in range(step):
                t = tt * step + i
                for n in range(2):
                    tile_load(n, t).wait()
                halfs[i] = nt(img[t], wc[t]).astype(BF16)
            for i in range(step):
                t = tt * step + i
                tile_load(2, t).wait()
                warped[t] = nn(wr[t], halfs[i]).astype(BF16)

    def combine(h, s):
        @pl.loop(0, NP)
        def _(p):
            ia, ib = tab_i[p], tab_i[NP + p]
            wa = jnp.full((16, 128), tab_w[p], F32).astype(BF16)
            wb = jnp.full((16, 128), tab_w[NP + p], F32).astype(BF16)
            bits = {}
            bits["y1"], bits["y0"] = gray(p // 4)
            bits["z1"], bits["z0"] = gray(p % 4)
            starts = []
            for k in range(6):
                place = 0
                for j in range(6):
                    d = ORDER[(k + j) % 6]
                    if d[0] != "x":
                        place = place + bits[d] * (32 >> j)
                starts.append(place * len(UNITS[s][k]) + UNITS[s][k][0] * 64)
            for xr in range(4):
                bits["x1"], bits["x0"] = gray(xr)
                for k in range(6):
                    shift = 0
                    for j in range(6):
                        d = ORDER[(k + j) % 6]
                        if d[0] == "x":
                            shift += bits[d] * (32 >> j)
                    for i, unit in enumerate(UNITS[s][k]):
                        rows = pl.ds(pl.multiple_of((xr * 2 + h) * 64 + unit % 4 * 16, 16), 16)
                        lanes = slice(unit // 4 * 128, unit // 4 * 128 + 128)
                        acc[h, starts[k] + shift * len(UNITS[s][k]) + i] = (
                            warped[ia, rows, lanes] * wa + warped[ib, rows, lanes] * wb
                        )

    def part(s, k, total, start, count):
        n = len(UNITS[s][k])
        return pl.ds(UNITS[s][k][0] * total + start * n, count * n)

    def core_copy(s, k):
        span = part(s, k, 64, 0, 64)
        return remote(acc.at[other, span], rc.at[span], csem_s.at[s, k], csem_r.at[s, k], mate)

    def core_start(s):
        for k in range(6):
            core_copy(s, k).start()

    def source_lines(q, first):
        return jnp.concatenate([metag[q, first + c : first + c + 1, :] for c in range(4)], axis=1)

    def measure(first, last):
        @pl.loop(first, last)
        def _(t):
            q = patch_sm[t]
            row_of = source_lines(q, 0)
            col_of = source_lines(q, 4)

            @pl.loop(0, 4)
            def _(b):
                start = pl.multiple_of(b * 128, 128)
                colt[pl.ds(start, 128), :] = profile(col_of, (b * 128).astype(F32), 128)

            def part(b, total):
                start = pl.multiple_of(b * 128, 128)
                by_col = nn(warped[t, pl.ds(start, 128), :], colt[...])
                rows = profile(row_of, (b * 128).astype(F32), 128).astype(F32)
                return total + jnp.sum((by_col * rows).reshape(16, 8, S), axis=0)

            total = lax.fori_loop(0, 4, part, jnp.zeros((8, S), F32))
            fluxo[pl.ds(t, 1), :] = jnp.sum(total, axis=0, keepdims=True)

    bufs = (r0, r1, r2)

    def base_of(k, j):
        if (k, j) in bases:
            return bases[k, j]
        base = 0
        for i in range(j):
            base = base + side[ORDER[(k + i) % 6]] * (32 >> i)
        return base

    def round_copy(s, k, j):
        d = ORDER[(k + j) % 6]
        half = 32 >> j
        start = base_of(k, j) + (1 - side[d]) * half
        src = acc.at[core, part(s, k, 64, start, half)]
        dst = bufs[j].at[part(s, k, half, 0, half)]
        return remote(src, dst, rsem_s.at[j, s * 6 + k], rsem_r.at[j, s * 6 + k], partner[d])

    def round_add(s, k, j):
        half = 32 >> j
        step = min(half, 16)

        @pl.loop(0, half // step)
        def _(i):
            at_ = part(s, k, 64, base_of(k, j + 1) + i * step, step)
            acc[core, at_] = acc[core, at_] + bufs[j][part(s, k, half, i * step, step)]

    def last_copy(s, k, e):
        place, there = lasts[k, e]
        return remote(
            acc.at[core, part(s, k, 64, place, 1)], fin.at[part(s, k, 8, e, 1)],
            fsem_s.at[s * 6 + k, e], fsem_r.at[s * 6 + k, e], there,
        )

    def core_add(s):
        for k in range(6):
            core_copy(s, k).wait()

            @pl.loop(0, 4)
            def _(i):
                at_ = part(s, k, 64, i * 16, 16)
                acc[core, at_] = acc[core, at_] + rc[at_]

            round_copy(s, k, 0).start()

    def advance(s, j):
        for k in range(6):
            round_copy(s, k, j).wait()
            round_add(s, k, j)
            if j < 2:
                round_copy(s, k, j + 1).start()
            else:
                for e in (7, 6, 5, 3, 4, 2, 1):
                    last_copy(s, k, e).start()

    def finish(s):
        for k in range(6):
            n = len(UNITS[s][k])
            place = base_of(k, 6)
            for e in (1, 2, 4, 3, 5, 6, 7):
                last_copy(s, k, e).wait()
            for i, unit in enumerate(UNITS[s][k]):
                value = acc[core, UNITS[s][k][0] * 64 + place * n + i].astype(F32)
                for e in range(1, 8):
                    value = value + fin[UNITS[s][k][0] * 8 + e * n + i].astype(F32)
                lanes = slice(unit // 4 * 128, unit // 4 * 128 + 128)
                sblk[unit % 4 * 16 : unit % 4 * 16 + 16, lanes] = value

    def tables():
        own_row = source_lines(me, 0)
        own_col = source_lines(me, 4)

        @pl.loop(0, 4)
        def _(b):
            start = pl.multiple_of(b * 128, 128)
            colt[pl.ds(start, 128), :] = profile(own_col, (b * 128).astype(F32), 128)
            rowt[pl.ds(start, 128), :] = profile(own_row, (b * 128).astype(F32), 128)

        load_r.wait()
        load_c.wait()

        @pl.loop(0, 4)
        def _(b):
            start = pl.multiple_of(b * 128, 128)
            cols = pl.ds(start, 128)
            high, low = split(mc[:, cols])
            value = tn(high, colt[...]) + tn(low, colt[...])
            bth[cols, :] = value.astype(BF16)
            high, low = split(mr[:, cols])
            at[cols, :] = tn(high, rowt[...]) + tn(low, rowt[...])
            high, low = split(mc[cols, :])
            mch[cols, :] = high
            mcl[cols, :] = low

    def rows_of(who):
        return pl.ds(pl.multiple_of(who * 64, 64), 64)

    own = rows_of(v)

    def share_copy(s, o):
        src = sg.at[s, own, :]
        where = mate if o == 0 else (((x + o) % 4) * 2 + core, me)
        return remote(src, src, asem_s.at[s, o], asem_r.at[s, o], where)

    def share_start(s):
        sg[s, own, :] = sblk[:, s * 256 : s * 256 + 256].astype(BF16)
        for o in (2, 1, 3, 0):
            share_copy(s, o).start()

    def came(s, o, base, half):
        rows = rows_of(((x - o + 4) % 4) * 2 + half)
        block = sg.at[s, rows, :]
        where = (((x + o) % 4) * 2 + core, me) if base == 0 else mate
        return remote(block, block, asem_s.at[s, base + o], asem_r.at[s, base + o], where)

    def share_pass(s):
        for o in (1, 3, 2):
            came(s, o, 0, core).wait()
            block = sg.at[s, rows_of(((x - o + 4) % 4) * 2 + core), :]
            remote(block, block, asem_s.at[s, 4 + o], asem_r.at[s, 4 + o], mate).start()

    def share_end(s):
        came(s, 0, 0, other).wait()
        for o in (1, 3, 2):
            came(s, o, 4, other).wait()

    def own_flux(s):
        cols = slice(s * 256, s * 256 + 256)
        high, low = split(sblk[:, cols])
        value = nn(jnp.concatenate([high, low], axis=0), bth[cols, :])
        return value[0:64] + value[64:128]

    warp(0, 6, 2)
    warp(6, TD, 1)
    pl.semaphore_wait(barrier, peers)
    combine(other, 0)
    core_start(0)
    gather_start(metag, 0)
    combine(other, 1)
    core_start(1)
    load_r.start()
    load_c.start()
    combine(core, 0)
    core_add(0)
    combine(core, 1)
    core_add(1)
    gather_wait(metag, 0)
    measure(0, 2)
    advance(0, 0)
    measure(2, 4)
    advance(1, 0)
    measure(4, 6)
    advance(0, 1)
    gather_start(infog, 3)
    measure(6, 7)
    advance(1, 1)
    measure(7, 8)
    fluxg[me] = fluxo[...].astype(BF16)
    tables()
    advance(0, 2)
    gather_wait(infog, 3)
    info = infog[...].reshape(128, 128)
    mine = (info == me.astype(F32)) & (lax.broadcasted_iota(jnp.int32, (128, 128), 1) < 64)
    weights = jnp.where(mine, pltpu.roll(info, 64, 1), 0.0)
    weight_sum = jnp.sum(jnp.sum(weights, axis=0, keepdims=True), axis=1, keepdims=True) * (1.0 / 64.0)
    pg[v, 4:5, :] = jnp.broadcast_to(weight_sum, (1, 128))
    pg[v, 5:8, :] = jnp.zeros((3, 128), F32)
    advance(1, 2)

    gather_start(fluxg, 1)
    finish(0)
    share_start(0)
    value[...] = own_flux(0)
    finish(1)
    share_start(1)
    partial = jnp.sum((value[...] + own_flux(1)) * at[own, :], axis=0, keepdims=True)
    for c in range(4):
        pg[v, c : c + 1, :] = partial[:, c * 128 : (c + 1) * 128]

    @pl.loop(1, NV)
    def _(o):
        remote(pg.at[v], pg.at[v], vsem_s.at[o], vsem_r.at[o], ((v + o) % NV, me)).start()

    share_pass(0)
    gather_wait(fluxg, 1)
    tile = lax.broadcasted_iota(jnp.int32, (128, 128), 0)
    lane = lax.broadcasted_iota(jnp.int32, (128, 128), 1)
    hits = (infog[...].reshape(128, 128) == (lane % 16).astype(F32)) & (tile % 4 == lane // 16)
    hits = jnp.where(hits, 1.0, 0.0).astype(BF16)
    sums[...] = tn(hits, fluxg[...].reshape(128, S))
    counts[...] = tn(hits, jnp.ones((128, 128), BF16))

    @pl.loop(1, NV)
    def _(o):
        theirs = (v - o + NV) % NV
        remote(pg.at[theirs], pg.at[theirs], vsem_s.at[o], vsem_r.at[o], ((v + o) % NV, me)).wait()

    total = jnp.sum(pg[...], axis=0)
    inverse = 1.0 / total[4:5, :]
    refg[me] = total * inverse
    gather_start(refg, 2)

    share_pass(1)
    mrow_high, mrow_low = split(mr[own, :])
    both = jnp.concatenate([mrow_high, mrow_low], axis=0)
    matched = jnp.zeros((64, S), F32)
    for s in range(2):
        share_end(s)
        cols = slice(s * 256, s * 256 + 256)
        half = nn(both, sg[s])
        high, low = split(half[0:64] + half[64:128])
        pair = nt(jnp.concatenate([high, low], axis=0), mch[:, cols])
        matched = matched + pair[0:64] + pair[64:128] + nt(high, mcl[:, cols])
    for c in range(4):
        coadd_ref[:, c * 128 : (c + 1) * 128] = matched[:, c * 128 : (c + 1) * 128] * inverse

    gather_wait(refg, 2)
    refs = jnp.concatenate([refg[:, c, :] for c in range(4)], axis=1)
    squares = jnp.sum(refs * refs, axis=1, keepdims=True)
    fits = []
    for u in range(4):
        rows = slice(u * 16, u * 16 + 16)
        top = jnp.sum(jnp.sum(sums[rows, :] * refs, axis=0, keepdims=True), axis=1, keepdims=True)
        low = jnp.sum(counts[rows, 0:1] * squares, axis=0, keepdims=True)
        fits.append(top / low)
    for u in range(4):
        zp_ref[u : u + 1, :] = jnp.broadcast_to(fits[u], (1, 128))
    for t in range(TD):
        q = patch_sm[t]
        template = jnp.concatenate([refg[q, c : c + 1, :] for c in range(4)], axis=1)
        resid_ref[t : t + 1, :] = fluxo[t : t + 1, :] - fits[t % 4] * template


def fused(tile_patch, tile_weight, images, warp_rows, warp_cols, match_rows, match_cols, src_row, src_col):
    dma = pltpu.SemaphoreType.DMA
    any_ = pl.BlockSpec(memory_space=pl.ANY)
    smem = pl.BlockSpec(memory_space=pltpu.SMEM)
    vmem = pl.BlockSpec(memory_space=pltpu.VMEM)
    return pl.pallas_call(
        kernel,
        out_shape=(
            jax.ShapeDtypeStruct((64, S), F32),
            jax.ShapeDtypeStruct((4, 128), F32),
            jax.ShapeDtypeStruct((TD, S), F32),
        ),
        in_specs=[smem, vmem, any_, any_, any_, any_, any_, vmem, vmem],
        out_specs=(vmem, vmem, vmem),
        scratch_shapes=[
            pltpu.VMEM((TD, S, S), BF16),
            pltpu.VMEM((TD, S, S), BF16),
            pltpu.VMEM((TD, S, S), BF16),
            pltpu.VMEM((2, S, S), BF16),
            pltpu.VMEM((TD, S, S), BF16),
            pltpu.VMEM((S, S), F32),
            pltpu.VMEM((S, S), F32),
            pltpu.VMEM((2, 64 * 16, 16, 128), BF16),
            pltpu.VMEM((64 * 16, 16, 128), BF16),
            pltpu.VMEM((32 * 16, 16, 128), BF16),
            pltpu.VMEM((16 * 16, 16, 128), BF16),
            pltpu.VMEM((8 * 16, 16, 128), BF16),
            pltpu.VMEM((8 * 16, 16, 128), BF16),
            pltpu.VMEM((128, S), F32),
            pltpu.VMEM((128, 128), F32),
            pltpu.VMEM((64, S), F32),
            pltpu.VMEM((NP, 8, 128), F32),
            pltpu.VMEM((NP, TD, 128), F32),
            pltpu.VMEM((NP, TD, S), BF16),
            pltpu.VMEM((TD, S), F32),
            pltpu.VMEM((NV, 8, 128), F32),
            pltpu.VMEM((NP, 8, 128), F32),
            pltpu.VMEM((2, S, 256), BF16),
            pltpu.VMEM((S, S), BF16),
            pltpu.VMEM((S, S), BF16),
            pltpu.VMEM((S, S), BF16),
            pltpu.VMEM((S, S), F32),
            pltpu.VMEM((S, S), BF16),
            pltpu.VMEM((S, S), BF16),
            pltpu.VMEM((64, S), F32),
            pltpu.SMEM((2 * NP,), jnp.int32),
            pltpu.SMEM((2 * NP,), F32),
            pltpu.SMEM((TD,), F32),
            dma((3, TD)), dma((3,)), dma((2, 6)), dma((2, 6)), dma((3, 12)), dma((3, 12)), dma((12, 8)), dma((12, 8)),
            dma((4, NP)), dma((4, NP)), dma((NV,)), dma((NV,)), dma((2, 8)), dma((2, 8)),
        ],
        compiler_params=pltpu.CompilerParams(
            collective_id=0, has_side_effects=True, vmem_limit_bytes=60 * 1024 * 1024
        ),
        name="coadd",
    )(tile_patch, tile_weight, images, warp_rows, warp_cols, match_rows, match_cols, src_row, src_col)


def store(coadd_in, zp_in, resid_in, coadd_ref, zp_ref, resid_ref):
    coadd_ref[0] = coadd_in[...]
    resid_ref[...] = resid_in[...]
    for u in range(4):
        zp_ref[u] = jnp.max(zp_in[u : u + 1, :])


def shards(
    images, warp_rows, warp_cols, tile_weight, tile_patch, match_rows, match_cols, src_row, src_col
):
    coadd, zero_point, resid = fused(
        tile_patch, tile_weight[None], images, warp_rows, warp_cols, match_rows[0], match_cols[0], src_row, src_col
    )
    vmem = pl.BlockSpec(memory_space=pltpu.VMEM)
    return pl.pallas_call(
        store,
        out_shape=(
            jax.ShapeDtypeStruct((1, 64, S), F32),
            jax.ShapeDtypeStruct((4,), F32),
            jax.ShapeDtypeStruct((TD, S), F32),
        ),
        in_specs=[vmem, vmem, vmem],
        out_specs=(vmem, pl.BlockSpec(memory_space=pltpu.SMEM), vmem),
        name="store",
    )(coadd, zero_point, resid)


def solution(mesh):
    in_specs = (
        P(("visit", "patch"), None, None),
        P(("visit", "patch"), None, None),
        P(("visit", "patch"), None, None),
        P(("visit", "patch")),
        P(("visit", "patch")),
        P("patch", None, None),
        P("patch", None, None),
        P("patch", None),
        P("patch", None),
    )
    out_specs = (P("patch", "visit", None), P("visit"), P(("visit", "patch"), None))
    return jax.shard_map(shards, mesh=mesh, in_specs=in_specs, out_specs=out_specs, check_vma=False)
```
